256 devices in a mesh: fsdp: 8 (over x, y_hi), frame: 32 (over y_lo, z, core).
Axes of the slice: x: 4, y: 4 (y_hi: 2, y_lo: 2; y = y_hi * 2 + y_lo), z: 8, core: 2. Of those that a mesh axis runs over, the one named last changes fastest.
Arguments:
- queries: bfloat16 [32, 1024, 1024], P('frame', 'fsdp'), may hold values from -5 to 5
- key_rows: bfloat16 [32, 1024, 1024], P('frame', 'fsdp'), may hold values from -5 to 5
- value_rows: bfloat16 [32, 1024, 1024], P('frame', 'fsdp'), may hold values from -6 to 6
- out_weight: bfloat16 [1024, 2048], P(('fsdp', 'frame')), may hold values from -0.75 to 0.75
- conv_weight: bfloat16 [31, 2048], replicated, may hold values from -1 to 1
- grad_out: bfloat16 [32, 1024, 2048], P('frame', 'fsdp'), may hold values from -6 to 6
Outputs:
- block_out: bfloat16 [32, 1024, 2048], P('frame', 'fsdp')
- grad_queries: bfloat16 [32, 1024, 1024], P('frame', 'fsdp')
- grad_keys: bfloat16 [32, 1024, 1024], P('frame', 'fsdp')
- grad_values: bfloat16 [32, 1024, 1024], P('frame', 'fsdp')
- weight_grad: float32 [1024, 2048], P(('fsdp', 'frame'))
- conv_grad: float32 [31, 2048], replicated
The draws below stay inside these ranges and needn't reach their ends.
All inputs are finite; a program needn't handle non-finite values.
Results may differ from the reference program's by a relative error of at most 0.014.
Values may be sent and summed in bfloat16 or wider, within the bound.
A program may use at most 128 MiB of HBM per device.

```python
import math
import jax
import jax.numpy as jnp
from jax import lax

D = 2048
HEADS = 8
HDIM = 128
KERNEL = 31
INNER = 1024
SPAN = 1024
SPANS = 32


def base_field(key):
    field = jnp.clip(1.5 * jax.random.normal(key, (SPANS, SPAN, INNER), jnp.float32), -5.0, 5.0)
    return field


def draw_queries(key, part):
    field = base_field(jax.random.fold_in(key, 1))
    return field.astype(jnp.bfloat16)


def draw_key_rows(key, part):
    field = base_field(jax.random.fold_in(key, 2))
    return field.astype(jnp.bfloat16)


def shard_levels(key, shape, cuts, smallest, top_value):
    def one(axis_at, parts):
        heights = jax.random.uniform(jax.random.fold_in(jax.random.fold_in(key, 6), axis_at), (parts,), jnp.float32, smallest / len(cuts), top_value / len(cuts))
        return jnp.repeat(jnp.exp(heights), shape[axis_at] // parts).reshape((-1,) + (1,) * (len(shape) - axis_at - 1))

    level = one(*cuts[0])
    for cut in cuts[1:]:
        level = level * one(*cut)
    return level


def scatter_about(stream_key, dims, deviation, bound, shards=(), kind=jnp.bfloat16):
    gain = shard_levels(stream_key, dims, shards, -0.22, 0.18) if shards else 1.0
    drawn = jax.random.normal(stream_key, dims, jnp.float32) * deviation * gain
    return jnp.minimum(jnp.maximum(drawn, -bound), bound).astype(kind)


def setup_inputs(seed: int = 0) -> dict:
    streams_of = jax.random.split(jax.random.key(seed), 7)
    return {
        "queries": draw_queries(jax.random.fold_in(streams_of[6], 71), 0),
        "key_rows": draw_key_rows(jax.random.fold_in(streams_of[6], 71), 0),
        "value_rows": scatter_about(streams_of[2], (SPANS, SPAN, INNER), 1.0, 6.0, ((0, 32), (1, 8))),
        "out_weight": scatter_about(streams_of[3], (INNER, D), (INNER // 16) ** -0.5, 0.75, ((0, 256),)),
        "conv_weight": scatter_about(streams_of[4], (KERNEL, D), KERNEL ** -0.5, 1.0),
        "grad_out": scatter_about(streams_of[5], (SPANS, SPAN, D), 1.0, 6.0, ((0, 32), (1, 8))),
    }


def reference(queries, key_rows, value_rows, out_weight, conv_weight, grad_out):
    inv_root = 1.0 / math.sqrt(HDIM)
    half_width = KERNEL // 2
    conv_taps = conv_weight.astype(jnp.float32)

    def one_span(running, inputs):
        span_q, span_k, span_v, span_g = inputs
        pieces = []
        kept_weights = []
        for head_index in range(HEADS):
            columns = slice(head_index * HDIM, (head_index + 1) * HDIM)
            scores = jnp.dot(span_q[:, columns], span_k[:, columns].T, preferred_element_type=jnp.float32) * inv_root
            row_max = lax.optimization_barrier(jnp.max(scores, axis=1))
            exponent = jnp.exp(scores - row_max[:, None])
            row_sum = lax.optimization_barrier(jnp.sum(exponent, axis=1))
            weights = exponent / row_sum[:, None]
            rounded = weights.astype(jnp.bfloat16)
            pieces.append(jnp.dot(rounded, span_v[:, columns], preferred_element_type=jnp.float32).astype(jnp.bfloat16))
            kept_weights.append(weights)
        attention = jnp.concatenate(pieces, axis=1)
        projected = jnp.dot(attention, out_weight, preferred_element_type=jnp.float32).astype(jnp.bfloat16)
        padded = jnp.pad(projected.astype(jnp.float32), ((half_width, half_width), (0, 0)))
        conv_value = jnp.zeros((SPAN, D), jnp.float32)
        for offset in range(KERNEL):
            conv_value = conv_value + conv_taps[offset] * padded[offset:offset + SPAN]
        sigmoid_conv = jax.nn.sigmoid(conv_value)
        block_out = (padded[half_width:half_width + SPAN] + conv_value * sigmoid_conv).astype(jnp.bfloat16)
        upstream = span_g.astype(jnp.float32)
        grad_conv = (upstream * sigmoid_conv * (1.0 + conv_value * (1.0 - sigmoid_conv))).astype(jnp.bfloat16)
        grad_padded = jnp.pad(grad_conv.astype(jnp.float32), ((half_width, half_width), (0, 0)))
        grad_sum = upstream
        for offset in range(KERNEL):
            start_row = 2 * half_width - offset
            grad_sum = grad_sum + conv_taps[offset] * grad_padded[start_row:start_row + SPAN]
        grad_projected = grad_sum.astype(jnp.bfloat16)
        conv_terms = jnp.stack([lax.optimization_barrier(jnp.sum(grad_conv.astype(jnp.float32) * padded[offset:offset + SPAN], axis=0)) for offset in range(KERNEL)])
        weight_terms = jnp.dot(attention.T, grad_projected, preferred_element_type=jnp.float32)
        grad_attention = jnp.dot(grad_projected, out_weight.T, preferred_element_type=jnp.float32).astype(jnp.bfloat16)
        query_list = []
        key_list = []
        value_list = []
        for head_index in range(HEADS):
            columns = slice(head_index * HDIM, (head_index + 1) * HDIM)
            weights = kept_weights[head_index]
            grad_head = grad_attention[:, columns]
            grad_probs = jnp.dot(grad_head, span_v[:, columns].T, preferred_element_type=jnp.float32)
            row_dot = lax.optimization_barrier(jnp.sum(weights * grad_probs, axis=1))
            grad_scores = (weights * (grad_probs - row_dot[:, None])).astype(jnp.bfloat16)
            query_list.append((jnp.dot(grad_scores, span_k[:, columns], preferred_element_type=jnp.float32) * inv_root).astype(jnp.bfloat16))
            key_list.append((jnp.dot(grad_scores.T, span_q[:, columns], preferred_element_type=jnp.float32) * inv_root).astype(jnp.bfloat16))
            value_list.append(jnp.dot(weights.astype(jnp.bfloat16).T, grad_head, preferred_element_type=jnp.float32).astype(jnp.bfloat16))
        outputs = (block_out, jnp.concatenate(query_list, axis=1), jnp.concatenate(key_list, axis=1), jnp.concatenate(value_list, axis=1))
        return ((running[0] + weight_terms, running[1] + conv_terms), outputs)
    start_sums = (jnp.zeros((INNER, D), jnp.float32), jnp.zeros((KERNEL, D), jnp.float32))
    sums_done, stacked = lax.scan(one_span, start_sums, (queries, key_rows, value_rows, grad_out))
    grad_scale = 1.0 / math.sqrt(SPAN * SPANS)
    return (stacked[0], stacked[1], stacked[2], stacked[3], sums_done[0] * grad_scale, sums_done[1] * grad_scale)
```

```python
import math

import jax
import jax.numpy as jnp
from jax import lax
from jax.experimental import pallas as pl
from jax.experimental.pallas import tpu as pltpu
from jax.sharding import PartitionSpec as P

MESH = pl.DeviceIdType.MESH
HDIM = 128
KERNEL = 31
ROWS = 128
INNER = 1024
D = 2048
SPAN = 1024
FS = 8
NZ = 8
NP = 16
HALO = 32
COLS = 256
BLK = 256
INV_ROOT = 1.0 / math.sqrt(HDIM)
EXP_SCALE = INV_ROOT * math.log2(math.e)
F32 = jnp.float32
BF16 = jnp.bfloat16


def mod(a, n):
    return lax.rem(a, jnp.int32(n))


def remote(src, dst, send, recv, device):
    return pltpu.make_async_remote_copy(
        src_ref=src, dst_ref=dst, send_sem=send, recv_sem=recv, device_id=device, device_id_type=MESH
    )


def loop(lower, upper, body):
    def step(i, carry):
        body(i)
        return carry

    lax.fori_loop(lower, upper, step, 0)


def at128(i):
    return pl.ds(pl.multiple_of(i * 128, 128), 128)


def at64(i):
    return pl.ds(pl.multiple_of(i * 64, 64), 64)


def dot_nt(a, b):
    return lax.dot_general(a, b, (((1,), (1,)), ((), ())), preferred_element_type=F32)


def dot_tn(a, b):
    return lax.dot_general(a, b, (((0,), (0,)), ((), ())), preferred_element_type=F32)


def kernel(
    q_ref, k_ref, v_ref, w_ref, taps_ref, go_ref,
    o_block, o_gq, o_gk, o_gv, o_wg, o_cg,
    qkvh, prob, ohp, attx, wpl, wtmp, wbuf, perm, attp, attt, gox, tapf, proj_s, gc_s, wgs,
    ga_acc, ga_s, gh, dh, dk_acc, dv_acc, pbuf, sbuf, rbuf, wgp_s, wgp_r,
    tapg, ta, tp_s, tp_r, tb, tc_s, tc,
    qkv_ss, qkv_rs, wpl_ss, wpl_rs, go_ss, go_rs, ag_ss, ag_rs, agp_ss, agp_rs, att_ss, att_rs,
    ga_ss, ga_rs, rsp_ss, rsp_rs, rs_ss, rs_rs, d_ss, d_rs, wgp_ss, wgp_rs,
    ta_ss, ta_rs, tp_ss, tp_rs, tb_ss, tb_rs, tc_ss, tc_rs,
):
    f = lax.axis_index("fsdp").astype(jnp.int32)
    r = lax.axis_index("frame").astype(jnp.int32)
    ylo = lax.div(r, jnp.int32(16))
    z = mod(lax.div(r, jnp.int32(2)), NZ)
    core = mod(r, 2)
    me = f * 2 + ylo

    def plane(p):
        return (lax.div(p, jnp.int32(2)), mod(p, 2) * 16 + z * 2 + core)

    def zline(other):
        return (f, ylo * 16 + other * 2 + core)

    partner = (f, ylo * 16 + z * 2 + 1 - core)

    barrier = pltpu.get_barrier_semaphore()

    def greet_plane(k):
        pl.semaphore_signal(barrier, inc=1, device_id=plane(mod(me + k, NP)), device_id_type=MESH)

    def greet_z(k):
        pl.semaphore_signal(barrier, inc=1, device_id=zline(mod(z + k, NZ)), device_id_type=MESH)

    loop(1, NP, greet_plane)
    loop(1, NZ, greet_z)
    pl.semaphore_signal(barrier, inc=1, device_id=partner, device_id_type=MESH)
    pl.semaphore_wait(barrier, NP - 1 + NZ - 1 + 1)

    def wpl_copy(k):
        return remote(w_ref, wpl.at[me], wpl_ss.at[k], wpl_rs.at[k], plane(mod(me + k, NP)))

    loop(1, NP, lambda k: wpl_copy(k).start())

    heads = ((q_ref, 0), (k_ref, 1), (v_ref, 2))

    def qkv_copy(k, source, slot):
        peer = mod(f + k, FS)
        return remote(
            source.at[:, at128(peer)], qkvh.at[slot, at128(f), :], qkv_ss.at[slot, k], qkv_rs.at[slot, k], (peer, r)
        )

    def qkv_start(k):
        for source, slot in heads:
            qkv_copy(k, source, slot).start()

    loop(1, FS, qkv_start)

    def go_down():
        return remote(go_ref.at[pl.ds(0, 16), :], gox.at[pl.ds(144, 16), :], go_ss.at[0], go_rs.at[0], (f - 1, r))

    def go_up():
        return remote(go_ref.at[pl.ds(112, 16), :], gox.at[pl.ds(0, 16), :], go_ss.at[1], go_rs.at[1], (f + 1, r))

    @pl.when(f > 0)
    def _():
        go_down().start()

    @pl.when(f < FS - 1)
    def _():
        go_up().start()

    for source, slot in heads:
        qkvh[slot, at128(f), :] = source[:, at128(f)]
    gox[16:144, :] = go_ref[...]

    @pl.when(f == 0)
    def _():
        gox[0:16, :] = jnp.zeros((16, D), BF16)

    @pl.when(f == FS - 1)
    def _():
        gox[144:160, :] = jnp.zeros((16, D), BF16)

    ohp[0:HALO, :] = jnp.zeros((HALO, HDIM), BF16)
    ohp[HALO + SPAN : HALO + SPAN + HALO, :] = jnp.zeros((HALO, HDIM), BF16)
    tapf[0:KERNEL, :] = taps_ref[...].astype(F32)
    wpl[me] = w_ref[...]

    def perm_rows(b):
        row = lax.broadcasted_iota(jnp.int32, (128, INNER), 0) + b * 128
        col = lax.broadcasted_iota(jnp.int32, (128, INNER), 1)
        at = ((col >> 2) & 15) * 64 + ((col >> 6) & 7) * 8 + (col >> 9) * 4 + (col & 3)
        perm[at128(b), :] = jnp.where(row == at, 1.0, 0.0).astype(BF16)

    loop(0, 8, perm_rows)

    def wpl_arrived(k):
        source = mod(me - k + NP, NP)
        remote(w_ref, wpl.at[source], wpl_ss.at[k], wpl_rs.at[k], plane(source)).wait_recv()

    loop(1, NP, wpl_arrived)
    for p in range(NP):
        wtmp[4 * p : 4 * p + 4, :] = wpl[p].astype(F32)

    def wblock(c, zz):
        return pl.ds(pl.multiple_of(c * 512 + zz * 64, 64), 64)

    wbuf[wblock(core, z), :] = wtmp[...].astype(BF16)

    up, down = zline(mod(z + 1, NZ)), zline(mod(z + NZ - 1, NZ))

    def ag_copy(way, s, part):
        block = mod(z - s + NZ, NZ) if way == 0 else mod(z + s, NZ)
        view = wbuf.at[wblock(core, block), pl.ds(part * 1024, 1024)]
        return remote(view, view, ag_ss.at[way, s, part], ag_rs.at[way, s, part], up if way == 0 else down)

    def ag_arrived(way, s, part):
        block = mod(z - 1 - s + NZ, NZ) if way == 0 else mod(z + 1 + s, NZ)
        view = wbuf.at[wblock(core, block), pl.ds(part * 1024, 1024)]
        remote(view, view, ag_ss.at[way, s, part], ag_rs.at[way, s, part], down if way == 0 else up).wait_recv()

    def agp_copy(k):
        view = wbuf.at[wblock(core, mod(z + k, NZ)), :]
        return remote(view, view, agp_ss.at[k], agp_rs.at[k], partner)

    def agp_arrived(k):
        view = wbuf.at[wblock(1 - core, mod(z + k, NZ)), :]
        remote(view, view, agp_ss.at[k], agp_rs.at[k], partner).wait_recv()

    for part in range(2):
        for way in range(2):
            ag_copy(way, 0, part).start()
    agp_copy(0).start()

    def ag_turn(s):
        for part in range(2):
            for way in range(2):
                ag_arrived(way, s, part)
                if s + 1 < 3 or part == way:
                    ag_copy(way, s + 1, part).start()
        agp_copy(NZ - 1 - s).start()
        agp_copy(1 + s).start()

    ag_turn(0)

    def qkv_arrived(k):
        source = mod(f - k + FS, FS)
        for ref, slot in heads:
            remote(
                ref.at[:, at128(source)], qkvh.at[slot, at128(source), :], qkv_ss.at[slot, k], qkv_rs.at[slot, k], (source, r)
            ).wait_recv()

    loop(1, FS, qkv_arrived)

    def attend(i):
        rows = pl.ds(pl.multiple_of(i * BLK, BLK), BLK)
        scores = dot_nt(qkvh[0, rows, :], qkvh[1])
        exponent = jnp.exp2((scores - jnp.max(scores, axis=1, keepdims=True)) * EXP_SCALE)
        rounded = (exponent * (1.0 / jnp.sum(exponent, axis=1, keepdims=True))).astype(BF16)
        prob[rows, :] = rounded
        attended = jnp.dot(rounded, qkvh[2], preferred_element_type=F32)
        ohp[pl.ds(pl.multiple_of(i * BLK + HALO, HALO), BLK), :] = attended.astype(BF16)

    loop(0, 2, attend)
    ag_turn(1)
    loop(2, 4, attend)

    def ext(i):
        return pl.ds(pl.multiple_of(i * ROWS, ROWS), ROWS + 2 * HALO)

    def att_copy(k):
        peer = mod(f + k, FS)
        return remote(ohp.at[ext(peer), :], attx.at[:, at128(f)], att_ss.at[k], att_rs.at[k], (peer, r))

    def att_arrived(k):
        source = mod(f - k + FS, FS)
        remote(ohp.at[ext(source), :], attx.at[:, at128(source)], att_ss.at[k], att_rs.at[k], (source, r)).wait_recv()

    loop(1, FS, lambda k: att_copy(k).start())
    attx[:, at128(f)] = ohp[ext(f), :]
    ag_turn(2)
    ag_arrived(0, 3, 0)
    ag_arrived(1, 3, 1)
    agp_copy(4).start()

    @pl.when(f < FS - 1)
    def _():
        remote(go_ref.at[pl.ds(0, 16), :], gox.at[pl.ds(144, 16), :], go_ss.at[0], go_rs.at[0], (f + 1, r)).wait_recv()

    @pl.when(f > 0)
    def _():
        remote(go_ref.at[pl.ds(112, 16), :], gox.at[pl.ds(0, 16), :], go_ss.at[1], go_rs.at[1], (f - 1, r)).wait_recv()

    loop(1, FS, att_arrived)
    attp[...] = jnp.dot(attx[...], perm[...], preferred_element_type=F32).astype(BF16)
    attt[...] = attp[HALO : HALO + ROWS, :].T
    loop(0, NZ, agp_arrived)
    ga_acc[...] = jnp.zeros((ROWS, INNER), F32)
    tapg[KERNEL : KERNEL + 1, :] = jnp.zeros((1, D), F32)

    def columns(c):
        cols = pl.ds(pl.multiple_of(c * COLS, COLS), COLS)
        weight = wbuf[:, cols]
        proj_s[...] = jnp.dot(attp[...], weight, preferred_element_type=F32).astype(BF16).astype(F32)
        for lane in range(COLS // 128):
            here = pl.ds(pl.multiple_of(c * COLS + lane * 128, 128), 128)
            local = slice(lane * 128, lane * 128 + 128)
            conv = jnp.zeros((160, 128), F32)
            for j in range(KERNEL):
                conv = conv + tapf[j : j + 1, here] * proj_s[1 + j : 161 + j, local]
            sig = jax.nn.sigmoid(conv)
            upstream = gox[:, here].astype(F32)
            o_block[:, here] = (proj_s[32:160, local] + conv[16:144] * sig[16:144]).astype(BF16)
            gc_s[:, local] = (upstream * sig * (1.0 + conv * (1.0 - sig))).astype(BF16).astype(F32)
            total = go_ref[:, here].astype(F32)
            for j in range(KERNEL):
                total = total + tapf[j : j + 1, here] * gc_s[31 - j : 159 - j, local]
            gp = total.astype(BF16)
            gc_own = gc_s[16:144, local]
            for j in range(KERNEL):
                tapg[j : j + 1, here] = jnp.sum(gc_own * proj_s[17 + j : 145 + j, local], axis=0, keepdims=True)
            wgs[:, here] = jnp.dot(attt[...], gp, preferred_element_type=F32).astype(BF16)
            ga_acc[...] += dot_nt(gp, wbuf[:, here])

    loop(0, D // COLS, columns)
    ga_s[...] = dot_nt(ga_acc[...].astype(BF16), perm[...]).astype(BF16)

    def ga_copy(k):
        peer = mod(f + k, FS)
        return remote(ga_s.at[:, at128(peer)], gh.at[at128(f), :], ga_ss.at[k], ga_rs.at[k], (peer, r))

    def ga_arrived(k):
        source = mod(f - k + FS, FS)
        remote(ga_s.at[:, at128(source)], gh.at[at128(source), :], ga_ss.at[k], ga_rs.at[k], (source, r)).wait_recv()

    loop(1, FS, lambda k: ga_copy(k).start())

    def rsp_copy(k):
        block = mod(z + k, NZ)
        return remote(wgs.at[wblock(1 - core, block), :], pbuf.at[at64(block), :], rsp_ss.at[k], rsp_rs.at[k], partner)

    def rsp_arrived(k):
        block = mod(z + k, NZ)
        remote(wgs.at[wblock(core, block), :], pbuf.at[at64(block), :], rsp_ss.at[k], rsp_rs.at[k], partner).wait_recv()

    for k in (7, 1, 6, 2, 5, 3, 4, 0):
        rsp_copy(k).start()

    def ta_copy(k):
        peer = mod(me + k, NP)
        return remote(tapg.at[:, at128(peer)], ta.at[k], ta_ss.at[k], ta_rs.at[k], plane(peer))

    def ta_arrived(k):
        source = mod(me - k + NP, NP)
        remote(tapg.at[:, at128(source)], ta.at[k], ta_ss.at[k], ta_rs.at[k], plane(source)).wait_recv()

    loop(1, NP, lambda k: ta_copy(k).start())
    gh[at128(f), :] = ga_s[:, at128(f)]

    def rs_copy(way, s, part):
        piece = pl.ds(part * 512, 512)
        return remote(
            sbuf.at[s, way, :, piece], rbuf.at[s, way, :, piece], rs_ss.at[s, way, part], rs_rs.at[s, way, part],
            up if way == 0 else down,
        )

    def rs_arrived(way, s, part):
        piece = pl.ds(part * 512, 512)
        remote(
            sbuf.at[s, way, :, piece], rbuf.at[s, way, :, piece], rs_ss.at[s, way, part], rs_rs.at[s, way, part],
            down if way == 0 else up,
        ).wait_recv()

    def chip_sum(block, cols):
        return wgs[wblock(core, block), cols].astype(F32) + pbuf[at64(block), cols].astype(F32)

    def rs_turn(s):
        if s < 4:
            rsp_arrived(NZ - 1 - s)
        if s < 3:
            rsp_arrived(1 + s)
        for part in range(2):
            for way in range(2):
                block = mod(z - 1 - s + NZ, NZ) if way == 0 else mod(z + 1 + s, NZ)
                piece = slice(part * 512, part * 512 + 512)
                value = chip_sum(block, slice(way * 1024 + part * 512, way * 1024 + part * 512 + 512))
                if s > 0:
                    rs_arrived(way, s - 1, part)
                    value = value + rbuf[s - 1, way, :, piece].astype(F32)
                sbuf[s, way, :, piece] = value.astype(BF16)
                rs_copy(way, s, part).start()

    rs_turn(0)
    loop(1, FS, ga_arrived)
    dk_acc[...] = jnp.zeros((SPAN, HDIM), F32)
    dv_acc[...] = jnp.zeros((SPAN, HDIM), F32)

    def attend_back(i):
        rows = pl.ds(pl.multiple_of(i * BLK, BLK), BLK)
        grad = gh[rows, :]
        rounded = prob[rows, :]
        weights = rounded.astype(F32)
        grad_probs = dot_nt(grad, qkvh[2])
        row_dot = jnp.sum(weights * grad_probs, axis=1, keepdims=True)
        grad_scores = (weights * (grad_probs - row_dot)).astype(BF16)
        dh[0, rows, :] = (jnp.dot(grad_scores, qkvh[1], preferred_element_type=F32) * INV_ROOT).astype(BF16)
        dk_acc[...] += dot_tn(grad_scores, qkvh[0, rows, :])
        dv_acc[...] += dot_tn(rounded, grad)

    def tp_copy():
        return remote(tp_s, tp_r, tp_ss, tp_rs, partner)

    def tb_copy(k):
        return remote(tb.at[z], tb.at[z], tb_ss.at[k], tb_rs.at[k], zline(mod(z + k, NZ)))

    def tb_arrived(k):
        source = mod(z - k + NZ, NZ)
        remote(tb.at[source], tb.at[source], tb_ss.at[k], tb_rs.at[k], zline(source)).wait_recv()

    def tc_copy(k):
        return remote(tc_s, tc.at[me], tc_ss.at[k], tc_rs.at[k], plane(mod(me + k, NP)))

    def tc_arrived(k):
        source = mod(me - k + NP, NP)
        remote(tc_s, tc.at[source], tc_ss.at[k], tc_rs.at[k], plane(source)).wait_recv()

    loop(0, 1, attend_back)
    loop(1, NP, ta_arrived)
    total = tapg[:, at128(me)]
    for k in range(1, NP):
        total = total + ta[k]
    tp_s[...] = total
    tp_copy().start()
    rs_turn(1)
    loop(1, 2, attend_back)
    tp_copy().wait_recv()
    tb[z] = tp_s[...] + tp_r[...]
    loop(1, NZ, lambda k: tb_copy(k).start())
    rs_turn(2)
    loop(2, 4, attend_back)
    dh[1] = (dk_acc[...] * INV_ROOT).astype(BF16)
    dh[2] = dv_acc[...].astype(BF16)

    outs = ((o_gq, 0), (o_gk, 1), (o_gv, 2))

    def d_copy(k, ref, slot):
        peer = mod(f + k, FS)
        return remote(dh.at[slot, at128(peer), :], ref.at[:, at128(f)], d_ss.at[slot, k], d_rs.at[slot, k], (peer, r))

    def d_start(k):
        for ref, slot in outs:
            d_copy(k, ref, slot).start()

    def d_arrived(k):
        source = mod(f - k + FS, FS)
        for ref, slot in outs:
            remote(
                dh.at[slot, at128(source), :], ref.at[:, at128(source)], d_ss.at[slot, k], d_rs.at[slot, k], (source, r)
            ).wait_recv()

    loop(1, FS, d_start)
    for ref, slot in outs:
        ref[:, at128(f)] = dh[slot, at128(f), :]
    rs_turn(3)
    loop(1, NZ, tb_arrived)
    total = tb[0]
    for k in range(1, NZ):
        total = total + tb[k]
    grad_scale = 1.0 / math.sqrt(SPAN * 32)
    tc_s[...] = total * grad_scale
    loop(1, NP, lambda k: tc_copy(k).start())
    tc[me] = tc_s[...]
    rs_turn(4)
    rs_turn(5)
    rs_turn(6)
    rsp_arrived(0)
    for part in range(2):
        for way in range(2):
            cols = slice(way * 1024 + part * 512, way * 1024 + part * 512 + 512)
            rs_arrived(way, 6, part)
            wtmp[:, cols] = chip_sum(z, cols) + rbuf[6, way, :, part * 512 : part * 512 + 512].astype(F32)
    for p in range(NP):
        wgp_s[p] = wtmp[4 * p : 4 * p + 4, :]

    def wgp_copy(k):
        peer = mod(me + k, NP)
        return remote(wgp_s.at[peer], wgp_r.at[k], wgp_ss.at[k], wgp_rs.at[k], plane(peer))

    def wgp_arrived(k):
        source = mod(me - k + NP, NP)
        remote(wgp_s.at[source], wgp_r.at[k], wgp_ss.at[k], wgp_rs.at[k], plane(source)).wait_recv()

    loop(1, NP, lambda k: wgp_copy(k).start())
    loop(1, NP, tc_arrived)
    for p in range(NP):
        o_cg[:, p * 128 : p * 128 + 128] = tc[p, 0:KERNEL, :]
    loop(1, FS, d_arrived)
    loop(1, NP, wgp_arrived)
    total = wgp_s[me]
    for k in range(1, NP):
        total = total + wgp_r[k]
    o_wg[...] = total * grad_scale

    def plane_sent(k):
        wpl_copy(k).wait_send()
        ta_copy(k).wait_send()
        tc_copy(k).wait_send()
        wgp_copy(k).wait_send()

    def span_sent(k):
        for ref, slot in heads:
            qkv_copy(k, ref, slot).wait_send()
        for ref, slot in outs:
            d_copy(k, ref, slot).wait_send()
        att_copy(k).wait_send()
        ga_copy(k).wait_send()

    loop(1, NP, plane_sent)
    loop(1, FS, span_sent)

    @pl.when(f > 0)
    def _():
        go_down().wait_send()

    @pl.when(f < FS - 1)
    def _():
        go_up().wait_send()

    for way in range(2):
        for part in range(2):
            for s in range(4):
                if s < 3 or part == way:
                    ag_copy(way, s, part).wait_send()
            for s in range(7):
                rs_copy(way, s, part).wait_send()

    def line_sent(k):
        agp_copy(k).wait_send()
        rsp_copy(k).wait_send()

    loop(0, NZ, line_sent)
    loop(1, NZ, lambda k: tb_copy(k).wait_send())
    tp_copy().wait_send()


def shards(queries, key_rows, value_rows, out_weight, conv_weight, grad_out):
    vmem = pl.BlockSpec(memory_space=pltpu.VMEM)
    dma = pltpu.SemaphoreType.DMA
    block_out, grad_queries, grad_keys, grad_values, weight_grad, conv_grad = pl.pallas_call(
        kernel,
        out_shape=(
            jax.ShapeDtypeStruct((ROWS, D), BF16),
            jax.ShapeDtypeStruct((ROWS, INNER), BF16),
            jax.ShapeDtypeStruct((ROWS, INNER), BF16),
            jax.ShapeDtypeStruct((ROWS, INNER), BF16),
            jax.ShapeDtypeStruct((4, D), F32),
            jax.ShapeDtypeStruct((KERNEL, D), F32),
        ),
        in_specs=[vmem] * 6,
        out_specs=(vmem,) * 6,
        scratch_shapes=[
            pltpu.VMEM((3, SPAN, HDIM), BF16),
            pltpu.VMEM((SPAN, SPAN), BF16),
            pltpu.VMEM((SPAN + 2 * HALO, HDIM), BF16),
            pltpu.VMEM((ROWS + 2 * HALO, INNER), BF16),
            pltpu.VMEM((NP, 4, D), BF16),
            pltpu.VMEM((64, D), F32),
            pltpu.VMEM((INNER, D), BF16),
            pltpu.VMEM((INNER, INNER), BF16),
            pltpu.VMEM((ROWS + 2 * HALO, INNER), BF16),
            pltpu.VMEM((INNER, ROWS), BF16),
            pltpu.VMEM((160, D), BF16),
            pltpu.VMEM((32, D), F32),
            pltpu.VMEM((ROWS + 2 * HALO, COLS), F32),
            pltpu.VMEM((160, COLS), F32),
            pltpu.VMEM((INNER, D), BF16),
            pltpu.VMEM((ROWS, INNER), F32),
            pltpu.VMEM((ROWS, INNER), BF16),
            pltpu.VMEM((SPAN, HDIM), BF16),
            pltpu.VMEM((3, SPAN, HDIM), BF16),
            pltpu.VMEM((SPAN, HDIM), F32),
            pltpu.VMEM((SPAN, HDIM), F32),
            pltpu.VMEM((512, D), BF16),
            pltpu.VMEM((7, 2, 64, 1024), BF16),
            pltpu.VMEM((7, 2, 64, 1024), BF16),
            pltpu.VMEM((NP, 4, D), F32),
            pltpu.VMEM((NP, 4, D), F32),
            pltpu.VMEM((32, D), F32),
            pltpu.VMEM((NP, 32, 128), F32),
            pltpu.VMEM((32, 128), F32),
            pltpu.VMEM((32, 128), F32),
            pltpu.VMEM((NZ, 32, 128), F32),
            pltpu.VMEM((32, 128), F32),
            pltpu.VMEM((NP, 32, 128), F32),
            dma((3, FS)), dma((3, FS)),
            dma((NP,)), dma((NP,)),
            dma((2,)), dma((2,)),
            dma((2, 4, 2)), dma((2, 4, 2)),
            dma((NZ,)), dma((NZ,)),
            dma((FS,)), dma((FS,)),
            dma((FS,)), dma((FS,)),
            dma((NZ,)), dma((NZ,)),
            dma((7, 2, 2)), dma((7, 2, 2)),
            dma((3, FS)), dma((3, FS)),
            dma((NP,)), dma((NP,)),
            dma((NP,)), dma((NP,)),
            dma, dma,
            dma((NZ,)), dma((NZ,)),
            dma((NP,)), dma((NP,)),
        ],
        compiler_params=pltpu.CompilerParams(
            collective_id=0, has_side_effects=True, vmem_limit_bytes=60 * 1024 * 1024
        ),
    )(queries[0], key_rows[0], value_rows[0], out_weight, conv_weight, grad_out[0])
    return (block_out[None], grad_queries[None], grad_keys[None], grad_values[None], weight_grad, conv_grad)


def solution(mesh):
    return jax.shard_map(
        shards,
        mesh=mesh,
        in_specs=(
            P("frame", "fsdp", None),
            P("frame", "fsdp", None),
            P("frame", "fsdp", None),
            P(("fsdp", "frame"), None),
            P(),
            P("frame", "fsdp", None),
        ),
        out_specs=(
            P("frame", "fsdp", None),
            P("frame", "fsdp", None),
            P("frame", "fsdp", None),
            P("frame", "fsdp", None),
            P(("fsdp", "frame"), None),
            P(),
        ),
        check_vma=False,
    )
```

```python
import math

import jax
import jax.numpy as jnp
from jax import lax
from jax.experimental import pallas as pl
from jax.experimental.pallas import tpu as pltpu
from jax.sharding import PartitionSpec as P

MESH = pl.DeviceIdType.MESH
HDIM = 128
KERNEL = 31
ROWS = 128
INNER = 1024
D = 2048
SPAN = 1024
FS = 8
NZ = 8
NP = 16
HALO = 32
COLS = 256
PART = 512
BLK = 256
INV_ROOT = 1.0 / math.sqrt(HDIM)
EXP_SCALE = INV_ROOT * math.log2(math.e)
F32 = jnp.float32
BF16 = jnp.bfloat16


def mod(a, n):
    return lax.rem(a, jnp.int32(n))


def remote(src, dst, send, recv, device):
    return pltpu.make_async_remote_copy(
        src_ref=src, dst_ref=dst, send_sem=send, recv_sem=recv, device_id=device, device_id_type=MESH
    )


def loop(lower, upper, body):
    def step(i, carry):
        body(i)
        return carry

    lax.fori_loop(lower, upper, step, 0)


def at128(i):
    return pl.ds(pl.multiple_of(i * 128, 128), 128)


def at64(i):
    return pl.ds(pl.multiple_of(i * 64, 64), 64)


def dot_nt(a, b):
    return lax.dot_general(a, b, (((1,), (1,)), ((), ())), preferred_element_type=F32)


def dot_tn(a, b):
    return lax.dot_general(a, b, (((0,), (0,)), ((), ())), preferred_element_type=F32)


def kernel(
    q_ref, k_ref, v_ref, w_ref, taps_ref, go_ref,
    o_block, o_gq, o_gk, o_gv, o_wg, o_cg,
    qkvh, prob, ohp, attx, wpl, wtmp, wbuf, perm, attp, attt, gox, tapv, tapb, proj_s, next_s, gc_s, gp_s, last_s, wgs,
    ga_acc, ga_s, gh, dh, dk_acc, dv_acc, pbuf, sbuf, rbuf, wgp_s, wgp_r,
    tapg, ta, tp_s, tp_r, tb, tc_s, tc,
    own_s, qkv_ss, qkv_rs, wpl_ss, wpl_rs, go_ss, go_rs, ag_ss, ag_rs, agp_ss, agp_rs, att_ss, att_rs,
    ga_ss, ga_rs, rsp_ss, rsp_rs, rs_ss, rs_rs, d_ss, d_rs, wgp_ss, wgp_rs,
    ta_ss, ta_rs, tp_ss, tp_rs, tb_ss, tb_rs, tc_ss, tc_rs,
):
    f = lax.axis_index("fsdp").astype(jnp.int32)
    r = lax.axis_index("frame").astype(jnp.int32)
    ylo = lax.div(r, jnp.int32(16))
    z = mod(lax.div(r, jnp.int32(2)), NZ)
    core = mod(r, 2)
    me = f * 2 + ylo

    def plane(p):
        return (lax.div(p, jnp.int32(2)), mod(p, 2) * 16 + z * 2 + core)

    def zline(other):
        return (f, ylo * 16 + other * 2 + core)

    partner = (f, ylo * 16 + z * 2 + 1 - core)

    heads = ((q_ref, 0), (k_ref, 1), (v_ref, 2))

    def own_copies():
        for source, slot in heads:
            yield pltpu.make_async_copy(source.at[:, at128(f)], qkvh.at[slot, at128(f), :], own_s.at[slot])
        yield pltpu.make_async_copy(go_ref, gox.at[pl.ds(16, ROWS), :], own_s.at[3])
        yield pltpu.make_async_copy(w_ref, wpl.at[me], own_s.at[4])
        yield pltpu.make_async_copy(taps_ref, tapv, own_s.at[5])

    barrier = pltpu.get_barrier_semaphore()

    def greet_plane(k):
        pl.semaphore_signal(barrier, inc=1, device_id=plane(mod(me + k, NP)), device_id_type=MESH)

    def greet_z(k):
        pl.semaphore_signal(barrier, inc=1, device_id=zline(mod(z + k, NZ)), device_id_type=MESH)

    loop(1, NP, greet_plane)
    loop(1, NZ, greet_z)
    pl.semaphore_signal(barrier, inc=1, device_id=partner, device_id_type=MESH)
    for copy in own_copies():
        copy.start()

    @pl.when(f == 0)
    def _():
        gox[0:16, :] = jnp.zeros((16, D), BF16)

    @pl.when(f == FS - 1)
    def _():
        gox[144:160, :] = jnp.zeros((16, D), BF16)

    ohp[0:HALO, :] = jnp.zeros((HALO, HDIM), BF16)
    ohp[HALO + SPAN : HALO + SPAN + HALO, :] = jnp.zeros((HALO, HDIM), BF16)

    def perm_rows(b):
        row = lax.broadcasted_iota(jnp.int32, (128, INNER), 0) + b * 128
        col = lax.broadcasted_iota(jnp.int32, (128, INNER), 1)
        at = ((col >> 2) & 15) * 64 + ((col >> 6) & 7) * 8 + (col >> 9) * 4 + (col & 3)
        perm[at128(b), :] = jnp.where(row == at, 1.0, 0.0).astype(BF16)

    loop(0, 8, perm_rows)
    for copy in own_copies():
        copy.wait()
    taps = tapv[...].astype(F32)
    for j in range(KERNEL):
        tapb[j] = jnp.broadcast_to(taps[j : j + 1, :], (8, D))
    pl.semaphore_wait(barrier, NP - 1 + NZ - 1 + 1)

    def wpl_copy(k):
        return remote(w_ref, wpl.at[me], wpl_ss.at[k], wpl_rs.at[k], plane(mod(me + k, NP)))

    loop(1, NP, lambda k: wpl_copy(k).start())

    def qkv_copy(k, source, slot):
        peer = mod(f + k, FS)
        return remote(
            source.at[:, at128(peer)], qkvh.at[slot, at128(f), :], qkv_ss.at[slot, k], qkv_rs.at[slot, k], (peer, r)
        )

    def go_down():
        return remote(go_ref.at[pl.ds(0, 16), :], gox.at[pl.ds(144, 16), :], go_ss.at[0], go_rs.at[0], (f - 1, r))

    def go_up():
        return remote(go_ref.at[pl.ds(112, 16), :], gox.at[pl.ds(0, 16), :], go_ss.at[1], go_rs.at[1], (f + 1, r))

    for source, slot in heads[1:] + heads[:1]:
        loop(1, FS, lambda k: qkv_copy(k, source, slot).start())

    @pl.when(f > 0)
    def _():
        go_down().start()

    @pl.when(f < FS - 1)
    def _():
        go_up().start()

    def wpl_arrived(k):
        source = mod(me - k + NP, NP)
        remote(w_ref, wpl.at[source], wpl_ss.at[k], wpl_rs.at[k], plane(source)).wait_recv()

    loop(1, NP, wpl_arrived)
    for p in range(NP):
        wtmp[4 * p : 4 * p + 4, :] = wpl[p].astype(F32)

    def wblock(c, zz):
        return pl.ds(pl.multiple_of(c * 512 + zz * 64, 64), 64)

    wbuf[wblock(core, z), :] = wtmp[...].astype(BF16)

    up, down = zline(mod(z + 1, NZ)), zline(mod(z + NZ - 1, NZ))

    def ag_part(part):
        return pl.ds(part * PART, PART)

    def ag_copy(way, s, part):
        block = mod(z - s + NZ, NZ) if way == 0 else mod(z + s, NZ)
        view = wbuf.at[wblock(core, block), ag_part(part)]
        return remote(view, view, ag_ss.at[way, s, part], ag_rs.at[way, s, part], up if way == 0 else down)

    def ag_arrived(way, s, part):
        block = mod(z - 1 - s + NZ, NZ) if way == 0 else mod(z + 1 + s, NZ)
        view = wbuf.at[wblock(core, block), ag_part(part)]
        remote(view, view, ag_ss.at[way, s, part], ag_rs.at[way, s, part], down if way == 0 else up).wait_recv()

    def agp_copy(k, pair):
        view = wbuf.at[wblock(core, mod(z + k, NZ)), pl.ds(pair * 1024, 1024)]
        return remote(view, view, agp_ss.at[pair, k], agp_rs.at[pair, k], partner)

    def agp_arrived(k, pair):
        view = wbuf.at[wblock(1 - core, mod(z + k, NZ)), pl.ds(pair * 1024, 1024)]
        remote(view, view, agp_ss.at[pair, k], agp_rs.at[pair, k], partner).wait_recv()

    def goes_far(way, s, part):
        return s < 3 or part % 2 == way

    def ag_first(pair):
        for part in (2 * pair, 2 * pair + 1):
            for way in range(2):
                ag_copy(way, 0, part).start()
        agp_copy(0, pair).start()

    def ag_turn(s, pair):
        for part in (2 * pair, 2 * pair + 1):
            for way in range(2):
                if goes_far(way, s, part):
                    ag_arrived(way, s, part)
                    if s < 3 and goes_far(way, s + 1, part):
                        ag_copy(way, s + 1, part).start()
        if s < 3:
            agp_copy(NZ - 1 - s, pair).start()
            agp_copy(1 + s, pair).start()
        else:
            agp_copy(4, pair).start()

    ag_first(0)
    ag_turn(0, 0)

    def head_arrived(source, ref, slot):
        k = mod(f - source + FS, FS)
        remote(
            ref.at[:, at128(source)], qkvh.at[slot, at128(source), :], qkv_ss.at[slot, k], qkv_rs.at[slot, k], (source, r)
        ).wait_recv()

    for ref, slot in heads[1:]:
        loop(1, FS, lambda k: head_arrived(mod(f - k + FS, FS), ref, slot))

    def ext(i):
        return pl.ds(pl.multiple_of(i * ROWS, ROWS), ROWS + 2 * HALO)

    def att_copy(k):
        peer = mod(f + k, FS)
        return remote(ohp.at[ext(peer), :], attx.at[:, at128(f)], att_ss.at[k], att_rs.at[k], (peer, r))

    first = lax.div(f, jnp.int32(2))

    def att_send(i):
        for half in range(2):
            peer = mod(2 * (first + i) - 1 + half + FS, FS)

            @pl.when(peer != f)
            def _():
                att_copy(mod(peer - f + FS, FS)).start()

    def attend(i):
        block = mod(first + i, SPAN // BLK)
        for half in range(2):
            source = 2 * block + half

            @pl.when(source != f)
            def _():
                head_arrived(source, *heads[0])

        rows = pl.ds(pl.multiple_of(block * BLK, BLK), BLK)
        scores = dot_nt(qkvh[0, rows, :], qkvh[1])
        exponent = jnp.exp2((scores - jnp.max(scores, axis=1, keepdims=True)) * EXP_SCALE)
        rounded = (exponent * (1.0 / jnp.sum(exponent, axis=1, keepdims=True))).astype(BF16)
        prob[rows, :] = rounded
        attended = jnp.dot(rounded, qkvh[2], preferred_element_type=F32)
        ohp[pl.ds(pl.multiple_of(block * BLK + HALO, HALO), BLK), :] = attended.astype(BF16)

        @pl.when(i > 0)
        def _():
            att_send(i)

    def att_arrived(k):
        source = mod(f - k + FS, FS)
        remote(ohp.at[ext(source), :], attx.at[:, at128(source)], att_ss.at[k], att_rs.at[k], (source, r)).wait_recv()

    loop(0, SPAN // BLK, attend)
    att_send(SPAN // BLK)
    attx[:, at128(f)] = ohp[ext(f), :]
    ag_turn(1, 0)
    ag_first(1)
    ag_turn(2, 0)
    ag_turn(0, 1)
    ag_turn(3, 0)
    ag_turn(1, 1)

    @pl.when(f < FS - 1)
    def _():
        remote(go_ref.at[pl.ds(0, 16), :], gox.at[pl.ds(144, 16), :], go_ss.at[0], go_rs.at[0], (f + 1, r)).wait_recv()

    @pl.when(f > 0)
    def _():
        remote(go_ref.at[pl.ds(112, 16), :], gox.at[pl.ds(0, 16), :], go_ss.at[1], go_rs.at[1], (f - 1, r)).wait_recv()

    loop(1, FS, att_arrived)
    attp[...] = jnp.dot(attx[...], perm[...], preferred_element_type=F32).astype(BF16)
    attt[...] = attp[HALO : HALO + ROWS, :].T
    loop(0, NZ, lambda k: agp_arrived(k, 0))
    ga_acc[...] = jnp.zeros((ROWS, INNER), F32)
    tapg[KERNEL : KERNEL + 1, :] = jnp.zeros((1, D), F32)

    def rsp_copy(part):
        cols = pl.ds(pl.multiple_of(part * PART, PART), PART)
        rows = pl.ds(pl.multiple_of((1 - core) * 512, 512), 512)
        return remote(wgs.at[rows, cols], pbuf.at[:, cols], rsp_ss.at[part], rsp_rs.at[part], partner)

    def rsp_arrived(part):
        cols = pl.ds(part * PART, PART)
        rows = pl.ds(pl.multiple_of(core * 512, 512), 512)
        remote(wgs.at[rows, cols], pbuf.at[:, cols], rsp_ss.at[part], rsp_rs.at[part], partner).wait_recv()

    def ta_copy(k):
        peer = mod(me + k, NP)
        return remote(tapg.at[:, at128(peer)], ta.at[k], ta_ss.at[k], ta_rs.at[k], plane(peer))

    def ta_arrived(k):
        source = mod(me - k + NP, NP)
        remote(tapg.at[:, at128(source)], ta.at[k], ta_ss.at[k], ta_rs.at[k], plane(source)).wait_recv()

    def takes_part(way, s, part):
        return s > 0 or (part % 2 == 1) == (way == 0)

    def rs_copy(way, s, part):
        view = (way, s, slice(None), pl.ds(part * PART, PART))
        return remote(
            sbuf.at[view], rbuf.at[view], rs_ss.at[way, s, part], rs_rs.at[way, s, part], up if way == 0 else down
        )

    def rs_arrived(way, s, part):
        view = (way, s, slice(None), pl.ds(part * PART, PART))
        remote(
            sbuf.at[view], rbuf.at[view], rs_ss.at[way, s, part], rs_rs.at[way, s, part], down if way == 0 else up
        ).wait_recv()

    def chip_sum(block, cols):
        return wgs[wblock(core, block), cols].astype(F32) + pbuf[at64(block), cols].astype(F32)

    def rs(s, part):
        cols = slice(part * PART, part * PART + PART)
        if s == 0:
            rsp_arrived(part)
        for way in range(2):
            if not takes_part(way, s, part):
                continue
            block = mod(z + 4 - s, NZ) if way == 0 else mod(z + 4 + s, NZ)
            value = chip_sum(block, cols)
            if s > 0 and takes_part(way, s - 1, part):
                rs_arrived(way, s - 1, part)
                value = value + rbuf[way, s - 1, :, cols].astype(F32)
            sbuf[way, s, :, cols] = value.astype(BF16)
            rs_copy(way, s, part).start()

    def at_cols(c):
        return pl.ds(pl.multiple_of(c * COLS, COLS), COLS)

    def project(c):
        next_s[...] = jnp.dot(attp[...], wbuf[:, at_cols(c)], preferred_element_type=F32).astype(BF16).astype(F32)

    def pull_back(c):
        gp = last_s[...]
        wgs[:, at_cols(c)] = jnp.dot(attt[...], gp, preferred_element_type=F32).astype(BF16)
        ga_acc[...] += dot_nt(gp, wbuf[:, at_cols(c)])

    events = {
        1: ((ag_turn, 2, 1),),
        2: ((ag_turn, 3, 1),),
        3: ((rs, 0, 0),),
        5: ((rs, 1, 0), (rs, 0, 1)),
        7: ((rs, 2, 0), (rs, 1, 1), (rs, 0, 2)),
    }

    def columns(c):
        project(jnp.minimum(c + 1, D // COLS - 1))
        pull_back(jnp.maximum(c - 1, 0))
        for lane in range(COLS // 128):
            here = pl.ds(pl.multiple_of(c * COLS + lane * 128, 128), 128)
            local = slice(lane * 128, lane * 128 + 128)
            conv = jnp.zeros((20, 8, 128), F32)
            for shift in range(8):
                moved = proj_s[shift : shift + 184, local]
                for j in range(KERNEL):
                    if (1 + j) % 8 == shift:
                        start = 1 + j - shift
                        conv = conv + tapb[j, :, here][None] * moved[start : start + 160].reshape(20, 8, 128)
            conv = conv.reshape(160, 128)
            sig = jax.nn.sigmoid(conv)
            upstream = gox[:, here].astype(F32)
            o_block[:, here] = (proj_s[32:160, local] + conv[16:144] * sig[16:144]).astype(BF16)
            gc_s[:, local] = (upstream * sig * (1.0 + conv * (1.0 - sig))).astype(BF16).astype(F32)
            total = gox[16:144, here].astype(F32).reshape(16, 8, 128)
            for shift in range(8):
                moved = gc_s[shift : shift + 152, local]
                for j in range(KERNEL):
                    if (31 - j) % 8 == shift:
                        start = 31 - j - shift
                        total = total + tapb[j, :, here][None] * moved[start : start + 128].reshape(16, 8, 128)
            gp_s[:, local] = total.reshape(128, 128).astype(BF16)
            gc_own = gc_s[16:144, local].reshape(16, 8, 128)
            for shift in range(8):
                moved = proj_s[shift : shift + 184, local]
                for j in range(KERNEL):
                    if (17 + j) % 8 == shift:
                        start = 17 + j - shift
                        partial = jnp.sum(gc_own * moved[start : start + 128].reshape(16, 8, 128), axis=0)
                        tapg[j : j + 1, here] = jnp.sum(partial, axis=0, keepdims=True)
        proj_s[...] = next_s[...]
        last_s[...] = gp_s[...]

        @pl.when((c > 0) & (mod(c, 2) == 0))
        def _():
            rsp_copy(lax.div(c, jnp.int32(2)) - 1).start()

        @pl.when(mod(c, 2) == 1)
        def _():
            for i in range(4):
                peer = lax.div(c, jnp.int32(2)) * 4 + i

                @pl.when(peer != me)
                def _():
                    ta_copy(mod(peer - me + NP, NP)).start()

        for at, calls in events.items():

            @pl.when(c == at)
            def _():
                for call, *given in calls:
                    call(*given)

        @pl.when(c == 2)
        def _():
            loop(0, NZ, lambda k: agp_arrived(k, 1))

    project(0)
    proj_s[...] = next_s[...]
    last_s[...] = jnp.zeros((ROWS, COLS), BF16)
    loop(0, D // COLS, columns)
    pull_back(D // COLS - 1)
    rsp_copy(3).start()
    ga_s[...] = dot_nt(ga_acc[...].astype(BF16), perm[...]).astype(BF16)

    def ga_copy(k):
        peer = mod(f + k, FS)
        return remote(ga_s.at[:, at128(peer)], gh.at[at128(f), :], ga_ss.at[k], ga_rs.at[k], (peer, r))

    def ga_arrived(k):
        source = mod(f - k + FS, FS)
        remote(ga_s.at[:, at128(source)], gh.at[at128(source), :], ga_ss.at[k], ga_rs.at[k], (source, r)).wait_recv()

    loop(1, FS, lambda k: ga_copy(k).start())

    gh[at128(f), :] = ga_s[:, at128(f)]
    rs(3, 0)
    rs(2, 1)
    rs(1, 2)
    rs(0, 3)
    loop(1, FS, ga_arrived)
    dk_acc[...] = jnp.zeros((SPAN, HDIM), F32)
    dv_acc[...] = jnp.zeros((SPAN, HDIM), F32)

    outs = ((o_gq, 0), (o_gk, 1), (o_gv, 2))

    def d_copy(k, ref, slot):
        peer = mod(f + k, FS)
        return remote(dh.at[slot, at128(peer), :], ref.at[:, at128(f)], d_ss.at[slot, k], d_rs.at[slot, k], (peer, r))

    def attend_back(i):
        i = mod(i + lax.div(f, jnp.int32(2)), SPAN // BLK)
        rows = pl.ds(pl.multiple_of(i * BLK, BLK), BLK)
        grad = gh[rows, :]
        rounded = prob[rows, :]
        weights = rounded.astype(F32)
        grad_probs = dot_nt(grad, qkvh[2])
        row_dot = jnp.sum(weights * grad_probs, axis=1, keepdims=True)
        grad_scores = (weights * (grad_probs - row_dot)).astype(BF16)
        dh[0, rows, :] = (jnp.dot(grad_scores, qkvh[1], preferred_element_type=F32) * INV_ROOT).astype(BF16)
        for half in range(2):
            peer = 2 * i + half

            @pl.when(peer != f)
            def _():
                d_copy(mod(peer - f + FS, FS), o_gq, 0).start()

        dk_acc[...] += dot_tn(grad_scores, qkvh[0, rows, :])
        dv_acc[...] += dot_tn(rounded, grad)

    def tp_copy():
        return remote(tp_s, tp_r, tp_ss, tp_rs, partner)

    def tb_copy(k):
        return remote(tb.at[z], tb.at[z], tb_ss.at[k], tb_rs.at[k], zline(mod(z + k, NZ)))

    def tb_arrived(k):
        source = mod(z - k + NZ, NZ)
        remote(tb.at[source], tb.at[source], tb_ss.at[k], tb_rs.at[k], zline(source)).wait_recv()

    def tc_copy(k):
        return remote(tc_s, tc.at[me], tc_ss.at[k], tc_rs.at[k], plane(mod(me + k, NP)))

    def tc_arrived(k):
        source = mod(me - k + NP, NP)
        remote(tc_s, tc.at[source], tc_ss.at[k], tc_rs.at[k], plane(source)).wait_recv()

    grad_scale = 1.0 / math.sqrt(SPAN * 32)

    def wgp_copy(half, k):
        peer = mod(me + k, NP)
        return remote(wgp_s.at[half, peer], wgp_r.at[half, k], wgp_ss.at[half, k], wgp_rs.at[half, k], plane(peer))

    def wgp_arrived(half, k):
        source = mod(me - k + NP, NP)
        remote(
            wgp_s.at[half, source], wgp_r.at[half, k], wgp_ss.at[half, k], wgp_rs.at[half, k], plane(source)
        ).wait_recv()

    def settle(half):
        for part in (2 * half, 2 * half + 1):
            cols = slice(part * PART, part * PART + PART)
            rs_arrived(0, 3, part)
            rs_arrived(1, 3, part)
            wtmp[:, cols] = chip_sum(z, cols) + rbuf[0, 3, :, cols].astype(F32) + rbuf[1, 3, :, cols].astype(F32)
        for p in range(NP):
            wgp_s[half, p] = wtmp[4 * p : 4 * p + 4, half * 1024 : half * 1024 + 1024].astype(BF16)
        loop(1, NP, lambda k: wgp_copy(half, k).start())

    loop(1, NP, ta_arrived)
    total = tapg[:, at128(me)]
    for k in range(1, NP):
        total = total + ta[k]
    tp_s[...] = total
    tp_copy().start()
    loop(0, 2, attend_back)
    rs(3, 1)
    rs(2, 2)
    rs(1, 3)
    tp_copy().wait_recv()
    tb[z] = tp_s[...] + tp_r[...]
    loop(1, NZ, lambda k: tb_copy(k).start())
    loop(2, 4, attend_back)
    dh[1] = (dk_acc[...] * INV_ROOT).astype(BF16)
    dh[2] = dv_acc[...].astype(BF16)

    def d_start(k):
        d_copy(k, o_gk, 1).start()
        d_copy(k, o_gv, 2).start()

    def d_arrived(k):
        source = mod(f - k + FS, FS)
        for ref, slot in outs:
            remote(
                dh.at[slot, at128(source), :], ref.at[:, at128(source)], d_ss.at[slot, k], d_rs.at[slot, k], (source, r)
            ).wait_recv()

    loop(1, FS, d_start)
    for ref, slot in outs:
        ref[:, at128(f)] = dh[slot, at128(f), :]
    rs(3, 2)
    rs(2, 3)
    loop(1, NZ, tb_arrived)
    total = tb[0]
    for k in range(1, NZ):
        total = total + tb[k]
    tc_s[...] = total * grad_scale
    loop(1, NP, lambda k: tc_copy(k).start())
    tc[me] = tc_s[...]
    settle(0)
    rs(3, 3)
    settle(1)
    loop(1, NP, tc_arrived)
    for p in range(NP):
        o_cg[:, p * 128 : p * 128 + 128] = tc[p, 0:KERNEL, :]
    loop(1, FS, d_arrived)
    for half in range(2):
        loop(1, NP, lambda k: wgp_arrived(half, k))
        total = wgp_s[half, me].astype(F32)
        for k in range(1, NP):
            total = total + wgp_r[half, k].astype(F32)
        o_wg[:, half * 1024 : half * 1024 + 1024] = total * grad_scale

    def plane_sent(k):
        wpl_copy(k).wait_send()
        ta_copy(k).wait_send()
        tc_copy(k).wait_send()
        for half in range(2):
            wgp_copy(half, k).wait_send()

    def span_sent(k):
        for ref, slot in heads:
            qkv_copy(k, ref, slot).wait_send()
        for ref, slot in outs:
            d_copy(k, ref, slot).wait_send()
        att_copy(k).wait_send()
        ga_copy(k).wait_send()

    loop(1, NP, plane_sent)
    loop(1, FS, span_sent)

    @pl.when(f > 0)
    def _():
        go_down().wait_send()

    @pl.when(f < FS - 1)
    def _():
        go_up().wait_send()

    for way in range(2):
        for s in range(4):
            for part in range(4):
                if goes_far(way, s, part):
                    ag_copy(way, s, part).wait_send()
                if takes_part(way, s, part):
                    rs_copy(way, s, part).wait_send()
    for part in range(4):
        rsp_copy(part).wait_send()
    for pair in range(2):
        loop(0, NZ, lambda k: agp_copy(k, pair).wait_send())
    loop(1, NZ, lambda k: tb_copy(k).wait_send())
    tp_copy().wait_send()


def put_out(*refs):
    sources, targets, rooms, into, out = refs[:6], refs[6:12], refs[12:18], refs[18], refs[19]
    loads = [pltpu.make_async_copy(sources[i], rooms[i], into.at[i]) for i in range(6)]
    stores = [pltpu.make_async_copy(rooms[i], targets[i], out.at[i]) for i in range(6)]
    for load in loads:
        load.start()
    for load, store in zip(loads, stores):
        load.wait()
        store.start()
    for store in stores:
        store.wait()


def shards(queries, key_rows, value_rows, out_weight, conv_weight, grad_out):
    vmem = pl.BlockSpec(memory_space=pltpu.VMEM)
    hbm = pl.BlockSpec(memory_space=pltpu.HBM)
    anywhere = pl.BlockSpec(memory_space=pl.ANY)
    dma = pltpu.SemaphoreType.DMA
    results = (
        ((ROWS, D), BF16),
        ((ROWS, INNER), BF16),
        ((ROWS, INNER), BF16),
        ((ROWS, INNER), BF16),
        ((4, D), F32),
        ((KERNEL, D), F32),
    )
    shapes = tuple(jax.ShapeDtypeStruct(*result) for result in results)
    found = pl.pallas_call(
        kernel,
        out_shape=shapes,
        in_specs=[hbm] * 6,
        out_specs=(vmem,) * 6,
        scratch_shapes=[
            pltpu.VMEM((3, SPAN, HDIM), BF16),
            pltpu.VMEM((SPAN, SPAN), BF16),
            pltpu.VMEM((SPAN + 2 * HALO, HDIM), BF16),
            pltpu.VMEM((ROWS + 2 * HALO, INNER), BF16),
            pltpu.VMEM((NP, 4, D), BF16),
            pltpu.VMEM((64, D), F32),
            pltpu.VMEM((INNER, D), BF16),
            pltpu.VMEM((INNER, INNER), BF16),
            pltpu.VMEM((ROWS + 2 * HALO, INNER), BF16),
            pltpu.VMEM((INNER, ROWS), BF16),
            pltpu.VMEM((160, D), BF16),
            pltpu.VMEM((KERNEL, D), BF16),
            pltpu.VMEM((KERNEL, 8, D), F32),
            pltpu.VMEM((ROWS + 2 * HALO, COLS), F32),
            pltpu.VMEM((ROWS + 2 * HALO, COLS), F32),
            pltpu.VMEM((160, COLS), F32),
            pltpu.VMEM((ROWS, COLS), BF16),
            pltpu.VMEM((ROWS, COLS), BF16),
            pltpu.VMEM((INNER, D), BF16),
            pltpu.VMEM((ROWS, INNER), F32),
            pltpu.VMEM((ROWS, INNER), BF16),
            pltpu.VMEM((SPAN, HDIM), BF16),
            pltpu.VMEM((3, SPAN, HDIM), BF16),
            pltpu.VMEM((SPAN, HDIM), F32),
            pltpu.VMEM((SPAN, HDIM), F32),
            pltpu.VMEM((512, D), BF16),
            pltpu.VMEM((2, 4, 64, D), BF16),
            pltpu.VMEM((2, 4, 64, D), BF16),
            pltpu.VMEM((2, NP, 4, 1024), BF16),
            pltpu.VMEM((2, NP, 4, 1024), BF16),
            pltpu.VMEM((32, D), F32),
            pltpu.VMEM((NP, 32, 128), F32),
            pltpu.VMEM((32, 128), F32),
            pltpu.VMEM((32, 128), F32),
            pltpu.VMEM((NZ, 32, 128), F32),
            pltpu.VMEM((32, 128), F32),
            pltpu.VMEM((NP, 32, 128), F32),
            dma((6,)),
            dma((3, FS)), dma((3, FS)),
            dma((NP,)), dma((NP,)),
            dma((2,)), dma((2,)),
            dma((2, 4, 4)), dma((2, 4, 4)),
            dma((2, NZ)), dma((2, NZ)),
            dma((FS,)), dma((FS,)),
            dma((FS,)), dma((FS,)),
            dma((4,)), dma((4,)),
            dma((2, 4, 4)), dma((2, 4, 4)),
            dma((3, FS)), dma((3, FS)),
            dma((2, NP)), dma((2, NP)),
            dma((NP,)), dma((NP,)),
            dma, dma,
            dma((NZ,)), dma((NZ,)),
            dma((NP,)), dma((NP,)),
        ],
        compiler_params=pltpu.CompilerParams(
            collective_id=0, has_side_effects=True, vmem_limit_bytes=50 * 1024 * 1024
        ),
    )(
        *(
            pltpu.with_memory_space_constraint(given, pltpu.HBM)
            for given in (queries[0], key_rows[0], value_rows[0], out_weight, conv_weight, grad_out[0])
        )
    )
    block_out, grad_queries, grad_keys, grad_values, weight_grad, conv_grad = pl.pallas_call(
        put_out,
        out_shape=shapes,
        in_specs=[anywhere] * 6,
        out_specs=(hbm,) * 6,
        scratch_shapes=[pltpu.VMEM(*result) for result in results] + [dma((6,)), dma((6,))],
        compiler_params=pltpu.CompilerParams(vmem_limit_bytes=8 * 1024 * 1024),
    )(*found)
    return (block_out[None], grad_queries[None], grad_keys[None], grad_values[None], weight_grad, conv_grad)


def solution(mesh):
    return jax.shard_map(
        shards,
        mesh=mesh,
        in_specs=(
            P("frame", "fsdp", None),
            P("frame", "fsdp", None),
            P("frame", "fsdp", None),
            P(("fsdp", "frame"), None),
            P(),
            P("frame", "fsdp", None),
        ),
        out_specs=(
            P("frame", "fsdp", None),
            P("frame", "fsdp", None),
            P("frame", "fsdp", None),
            P("frame", "fsdp", None),
            P(("fsdp", "frame"), None),
            P(),
        ),
        check_vma=False,
    )
```

```python
import math

import jax
import jax.numpy as jnp
from jax import lax
from jax.experimental import pallas as pl
from jax.experimental.pallas import tpu as pltpu
from jax.sharding import PartitionSpec as P

MESH = pl.DeviceIdType.MESH
HDIM = 128
KERNEL = 31
ROWS = 128
INNER = 1024
D = 2048
SPAN = 1024
FS = 8
NZ = 8
NP = 16
HALO = 32
COLS = 256
PART = 512
BLK = 256
INV_ROOT = 1.0 / math.sqrt(HDIM)
EXP_SCALE = INV_ROOT * math.log2(math.e)
F32 = jnp.float32
BF16 = jnp.bfloat16


def mod(a, n):
    return lax.rem(a, jnp.int32(n))


def remote(src, dst, send, recv, device):
    return pltpu.make_async_remote_copy(
        src_ref=src, dst_ref=dst, send_sem=send, recv_sem=recv, device_id=device, device_id_type=MESH
    )


def loop(lower, upper, body):
    def step(i, carry):
        body(i)
        return carry

    lax.fori_loop(lower, upper, step, 0)


def at128(i):
    return pl.ds(pl.multiple_of(i * 128, 128), 128)


def at64(i):
    return pl.ds(pl.multiple_of(i * 64, 64), 64)


def dot_nt(a, b):
    return lax.dot_general(a, b, (((1,), (1,)), ((), ())), preferred_element_type=F32)


def dot_tn(a, b):
    return lax.dot_general(a, b, (((0,), (0,)), ((), ())), preferred_element_type=F32)


def kernel(
    q_ref, k_ref, v_ref, w_ref, taps_ref, go_ref,
    o_block, o_gq, o_gk, o_gv, o_wg, o_cg,
    qkvh, prob, ohp, attx, wpl, wtmp, wbuf, perm, attp, attt, gox, tapv, tapb, proj_s, next_s, proj_all, gc_s, gc_all, gp_s, last_s, wgs,
    ga_acc, ga_s, gh, dh, dk_acc, dv_acc, pbuf, sbuf, rbuf, wgp_s, wgp_r,
    tapg, ta, tp_s, tp_r, tb, tc_s, tc,
    own_s, qkv_ss, q_rs, kv_rs, wpl_ss, wpl_rs, go_ss, go_rs, ag_ss, ag_rs, agp_ss, agp_rs, att_ss, att_rs,
    ga_ss, ga_rs, rsp_ss, rsp_rs, rs_ss, rs_rs, d_ss, d_rs, wgp_ss, wgp_rs,
    ta_ss, ta_rs, tp_ss, tp_rs, tb_ss, tb_rs, tc_ss, tc_rs,
):
    f = lax.axis_index("fsdp").astype(jnp.int32)
    r = lax.axis_index("frame").astype(jnp.int32)
    ylo = lax.div(r, jnp.int32(16))
    z = mod(lax.div(r, jnp.int32(2)), NZ)
    core = mod(r, 2)
    me = f * 2 + ylo

    def plane(p):
        return (lax.div(p, jnp.int32(2)), mod(p, 2) * 16 + z * 2 + core)

    def zline(other):
        return (f, ylo * 16 + other * 2 + core)

    partner = (f, ylo * 16 + z * 2 + 1 - core)

    def all_arrived(ref, sem):
        remote(ref, ref, sem, sem, partner).wait_recv()

    def all_sent(ref, sem):
        remote(ref, ref, sem, sem, partner).wait_send()

    heads = ((q_ref, 0), (k_ref, 1), (v_ref, 2))

    def own_copies():
        for source, slot in heads:
            yield pltpu.make_async_copy(source.at[:, at128(f)], qkvh.at[slot, at128(f), :], own_s.at[slot])
        yield pltpu.make_async_copy(go_ref, gox.at[pl.ds(16, ROWS), :], own_s.at[3])
        yield pltpu.make_async_copy(w_ref, wpl.at[me], own_s.at[4])
        yield pltpu.make_async_copy(taps_ref, tapv, own_s.at[5])

    barrier = pltpu.get_barrier_semaphore()

    def greet_plane(k):
        pl.semaphore_signal(barrier, inc=1, device_id=plane(mod(me + k, NP)), device_id_type=MESH)

    def greet_z(k):
        pl.semaphore_signal(barrier, inc=1, device_id=zline(mod(z + k, NZ)), device_id_type=MESH)

    loop(1, NP, greet_plane)
    loop(1, NZ, greet_z)
    pl.semaphore_signal(barrier, inc=1, device_id=partner, device_id_type=MESH)
    for copy in own_copies():
        copy.start()

    @pl.when(f == 0)
    def _():
        gox[0:16, :] = jnp.zeros((16, D), BF16)

    @pl.when(f == FS - 1)
    def _():
        gox[144:160, :] = jnp.zeros((16, D), BF16)

    ohp[0:HALO, :] = jnp.zeros((HALO, HDIM), BF16)
    ohp[HALO + SPAN : HALO + SPAN + HALO, :] = jnp.zeros((HALO, HDIM), BF16)

    def perm_rows(b):
        row = lax.broadcasted_iota(jnp.int32, (128, INNER), 0) + b * 128
        col = lax.broadcasted_iota(jnp.int32, (128, INNER), 1)
        at = ((col >> 2) & 15) * 64 + ((col >> 6) & 7) * 8 + (col >> 9) * 4 + (col & 3)
        perm[at128(b), :] = jnp.where(row == at, 1.0, 0.0).astype(BF16)

    loop(0, 8, perm_rows)
    for copy in own_copies():
        copy.wait()
    taps = tapv[...].astype(F32)
    for j in range(KERNEL):
        tapb[j] = jnp.broadcast_to(taps[j : j + 1, :], (8, D))
    pl.semaphore_wait(barrier, NP - 1 + NZ - 1 + 1)

    def wpl_copy(k):
        return remote(w_ref, wpl.at[me], wpl_ss, wpl_rs, plane(mod(me + k, NP)))

    loop(1, NP, lambda k: wpl_copy(k).start())

    def qkv_copy(k, source, slot):
        peer = mod(f + k, FS)
        arrival = q_rs.at[k] if slot == 0 else kv_rs.at[slot - 1]
        return remote(source.at[:, at128(peer)], qkvh.at[slot, at128(f), :], qkv_ss, arrival, (peer, r))

    def go_down():
        return remote(go_ref.at[pl.ds(0, 16), :], gox.at[pl.ds(144, 16), :], go_ss.at[0], go_rs.at[0], (f - 1, r))

    def go_up():
        return remote(go_ref.at[pl.ds(112, 16), :], gox.at[pl.ds(0, 16), :], go_ss.at[1], go_rs.at[1], (f + 1, r))

    loop(1, FS, lambda k: qkv_copy(k, k_ref, 1).start())
    all_arrived(wpl.at[pl.ds(0, NP - 1)], wpl_rs)
    for p in range(NP):
        wtmp[4 * p : 4 * p + 4, :] = wpl[p].astype(F32)

    def wblock(c, zz):
        return pl.ds(pl.multiple_of(c * 512 + zz * 64, 64), 64)

    wbuf[wblock(core, z), :] = wtmp[...].astype(BF16)

    up, down = zline(mod(z + 1, NZ)), zline(mod(z + NZ - 1, NZ))

    def ag_part(part):
        return pl.ds(part * PART, PART)

    def ag_copy(way, s, part):
        block = mod(z - s + NZ, NZ) if way == 0 else mod(z + s, NZ)
        view = wbuf.at[wblock(core, block), ag_part(part)]
        return remote(view, view, ag_ss, ag_rs.at[way, s, part], up if way == 0 else down)

    def ag_arrived(way, s, part):
        block = mod(z - 1 - s + NZ, NZ) if way == 0 else mod(z + 1 + s, NZ)
        view = wbuf.at[wblock(core, block), ag_part(part)]
        remote(view, view, ag_ss, ag_rs.at[way, s, part], down if way == 0 else up).wait_recv()

    def agp_copy(k, part):
        view = wbuf.at[wblock(core, mod(z + k, NZ)), ag_part(part)]
        return remote(view, view, agp_ss, agp_rs.at[part], partner)

    def goes_far(way, s, part):
        return s < 3 or part % 2 == way

    def ag_first(*parts):
        for part in parts:
            for way in range(2):
                ag_copy(way, 0, part).start()
        for part in parts:
            agp_copy(0, part).start()

    def ag_turn(s, *parts):
        for part in parts:
            for way in range(2):
                if goes_far(way, s, part):
                    ag_arrived(way, s, part)
                    if s < 3 and goes_far(way, s + 1, part):
                        ag_copy(way, s + 1, part).start()
            if s < 3:
                agp_copy(NZ - 1 - s, part).start()
                agp_copy(1 + s, part).start()
            else:
                agp_copy(4, part).start()

    def agp_arrived(part):
        all_arrived(wbuf.at[pl.ds(0, 512), ag_part(part)], agp_rs.at[part])

    ag_first(0, 1, 2)
    loop(1, FS, lambda k: qkv_copy(k, v_ref, 2).start())
    loop(1, FS, lambda k: qkv_copy(k, q_ref, 0).start())

    @pl.when(f > 0)
    def _():
        go_down().start()

    @pl.when(f < FS - 1)
    def _():
        go_up().start()

    ag_turn(0, 0, 1, 2)

    def query_arrived(source):
        arrival = q_rs.at[mod(f - source + FS, FS)]
        remote(q_ref.at[:, at128(source)], qkvh.at[0, at128(source), :], qkv_ss, arrival, (source, r)).wait_recv()

    for slot in (1, 2):
        all_arrived(qkvh.at[slot, pl.ds(0, 896), :], kv_rs.at[slot - 1])

    def ext(i):
        return pl.ds(pl.multiple_of(i * ROWS, ROWS), ROWS + 2 * HALO)

    def att_copy(k):
        peer = mod(f + k, FS)
        return remote(ohp.at[ext(peer), :], attx.at[:, at128(f)], att_ss, att_rs, (peer, r))

    first = lax.div(f, jnp.int32(2))

    def att_send(i):
        for half in range(2):
            peer = mod(2 * (first + i) - 1 + half + FS, FS)

            @pl.when(peer != f)
            def _():
                att_copy(mod(peer - f + FS, FS)).start()

    def attend(i):
        block = mod(first + i, SPAN // BLK)
        for half in range(2):
            source = 2 * block + half

            @pl.when(source != f)
            def _():
                query_arrived(source)

        rows = pl.ds(pl.multiple_of(block * BLK, BLK), BLK)
        scores = dot_nt(qkvh[0, rows, :], qkvh[1])
        exponent = jnp.exp2((scores - jnp.max(scores, axis=1, keepdims=True)) * EXP_SCALE)
        rounded = (exponent * (1.0 / jnp.sum(exponent, axis=1, keepdims=True))).astype(BF16)
        prob[rows, :] = rounded
        attended = jnp.dot(rounded, qkvh[2], preferred_element_type=F32)
        ohp[pl.ds(pl.multiple_of(block * BLK + HALO, HALO), BLK), :] = attended.astype(BF16)

        @pl.when(i > 0)
        def _():
            att_send(i)

        for part in range(3):

            @pl.when(i == part)
            def _():
                ag_turn(1, part)

    loop(0, SPAN // BLK, attend)
    att_send(SPAN // BLK)
    attx[:, at128(f)] = ohp[ext(f), :]
    ag_turn(2, 0, 1, 2)
    ag_first(3)
    ag_turn(3, 0, 1, 2)
    ag_turn(0, 3)

    @pl.when(f < FS - 1)
    def _():
        remote(go_ref.at[pl.ds(0, 16), :], gox.at[pl.ds(144, 16), :], go_ss.at[0], go_rs.at[0], (f + 1, r)).wait_recv()

    @pl.when(f > 0)
    def _():
        remote(go_ref.at[pl.ds(112, 16), :], gox.at[pl.ds(0, 16), :], go_ss.at[1], go_rs.at[1], (f - 1, r)).wait_recv()

    all_arrived(attx.at[:, pl.ds(0, 896)], att_rs)
    attp[...] = jnp.dot(attx[...], perm[...], preferred_element_type=F32).astype(BF16)
    attt[...] = attp[HALO : HALO + ROWS, :].T
    agp_arrived(0)
    ga_acc[...] = jnp.zeros((ROWS, INNER), F32)
    tapg[KERNEL : KERNEL + 1, :] = jnp.zeros((1, D), F32)

    def rsp_copy(part):
        cols = pl.ds(pl.multiple_of(part * PART, PART), PART)
        rows = pl.ds(pl.multiple_of((1 - core) * 512, 512), 512)
        return remote(wgs.at[rows, cols], pbuf.at[:, cols], rsp_ss, rsp_rs.at[part], partner)

    def rsp_arrived(part):
        cols = pl.ds(part * PART, PART)
        rows = pl.ds(pl.multiple_of(core * 512, 512), 512)
        remote(wgs.at[rows, cols], pbuf.at[:, cols], rsp_ss, rsp_rs.at[part], partner).wait_recv()

    def ta_copy(k):
        peer = mod(me + k, NP)
        return remote(tapg.at[:, at128(peer)], ta.at[k], ta_ss, ta_rs, plane(peer))

    def takes_part(way, s, part):
        return s > 0 or (part % 2 == 1) == (way == 0)

    def rs_copy(way, s, part):
        view = (way, s, slice(None), pl.ds(part * PART, PART))
        return remote(
            sbuf.at[view], rbuf.at[view], rs_ss, rs_rs.at[way, s, part], up if way == 0 else down
        )

    def rs_arrived(way, s, part):
        view = (way, s, slice(None), pl.ds(part * PART, PART))
        remote(
            sbuf.at[view], rbuf.at[view], rs_ss, rs_rs.at[way, s, part], down if way == 0 else up
        ).wait_recv()

    def chip_sum(block, cols):
        return wgs[wblock(core, block), cols].astype(F32) + pbuf[at64(block), cols].astype(F32)

    def rs(s, part):
        cols = slice(part * PART, part * PART + PART)
        if s == 0:
            rsp_arrived(part)
        for way in range(2):
            if not takes_part(way, s, part):
                continue
            block = mod(z + 4 - s, NZ) if way == 0 else mod(z + 4 + s, NZ)
            value = chip_sum(block, cols)
            if s > 0 and takes_part(way, s - 1, part):
                rs_arrived(way, s - 1, part)
                value = value + rbuf[way, s - 1, :, cols].astype(F32)
            sbuf[way, s, :, cols] = value.astype(BF16)
            rs_copy(way, s, part).start()

    def at_cols(c):
        return pl.ds(pl.multiple_of(c * COLS, COLS), COLS)

    def project(c):
        next_s[...] = jnp.dot(attp[...], wbuf[:, at_cols(c)], preferred_element_type=F32).astype(BF16).astype(F32)

    def pull_back(c):
        gp = last_s[...]
        wgs[:, at_cols(c)] = jnp.dot(attt[...], gp, preferred_element_type=F32).astype(BF16)
        ga_acc[...] += dot_nt(gp, wbuf[:, at_cols(c)])

    events = {
        0: ((ag_turn, 1, 3), (agp_arrived, 1)),
        2: ((ag_turn, 2, 3), (agp_arrived, 2)),
        3: ((rs, 0, 0),),
        4: ((ag_turn, 3, 3), (agp_arrived, 3)),
        5: ((rs, 0, 1),),
        6: ((rs, 1, 0),),
        7: ((rs, 0, 2),),
    }

    def tap_grads(tile):
        here = at128(tile)
        gc_own = gc_all[:, here].reshape(16, 8, 128)
        for shift in range(8):
            moved = proj_all[shift : shift + 184, here]
            for j in range(KERNEL):
                if (17 + j) % 8 == shift:
                    start = 17 + j - shift
                    partial = jnp.sum(gc_own * moved[start : start + 128].reshape(16, 8, 128), axis=0)
                    tapg[j : j + 1, here] = jnp.sum(partial, axis=0, keepdims=True)

        @pl.when(tile != me)
        def _():
            ta_copy(mod(tile - me + NP, NP)).start()

    def columns(c):
        project(jnp.minimum(c + 1, D // COLS - 1))
        pull_back(jnp.maximum(c - 1, 0))
        for lane in range(COLS // 128):
            here = pl.ds(pl.multiple_of(c * COLS + lane * 128, 128), 128)
            local = slice(lane * 128, lane * 128 + 128)
            conv = jnp.zeros((20, 8, 128), F32)
            for shift in range(8):
                moved = proj_s[shift : shift + 184, local]
                for j in range(KERNEL):
                    if (1 + j) % 8 == shift:
                        start = 1 + j - shift
                        conv = conv + tapb[j, :, here][None] * moved[start : start + 160].reshape(20, 8, 128)
            conv = conv.reshape(160, 128)
            sig = jax.nn.sigmoid(conv)
            upstream = gox[:, here].astype(F32)
            o_block[:, here] = (proj_s[32:160, local] + conv[16:144] * sig[16:144]).astype(BF16)
            grad_conv = (upstream * sig * (1.0 + conv * (1.0 - sig))).astype(BF16).astype(F32)
            gc_s[:, local] = grad_conv
            gc_all[:, here] = grad_conv[16:144]
            total = gox[16:144, here].astype(F32).reshape(16, 8, 128)
            for shift in range(8):
                moved = gc_s[shift : shift + 152, local]
                for j in range(KERNEL):
                    if (31 - j) % 8 == shift:
                        start = 31 - j - shift
                        total = total + tapb[j, :, here][None] * moved[start : start + 128].reshape(16, 8, 128)
            gp_s[:, local] = total.reshape(128, 128).astype(BF16)
        proj_all[:, at_cols(c)] = proj_s[...]
        proj_s[...] = next_s[...]
        last_s[...] = gp_s[...]

        @pl.when((c > 0) & (mod(c, 2) == 0))
        def _():
            rsp_copy(lax.div(c, jnp.int32(2)) - 1).start()

        for at, calls in events.items():

            @pl.when(c == at)
            def _():
                for call, *given in calls:
                    call(*given)

    project(0)
    proj_s[...] = next_s[...]
    last_s[...] = jnp.zeros((ROWS, COLS), BF16)
    loop(0, D // COLS, columns)
    pull_back(D // COLS - 1)
    rsp_copy(3).start()
    ga_s[...] = dot_nt(ga_acc[...].astype(BF16), perm[...]).astype(BF16)

    def ga_copy(k):
        peer = mod(f + k, FS)
        return remote(ga_s.at[:, at128(peer)], gh.at[at128(f), :], ga_ss, ga_rs, (peer, r))

    loop(1, FS, lambda k: ga_copy(k).start())

    gh[at128(f), :] = ga_s[:, at128(f)]
    loop(0, 4, tap_grads)
    rs(2, 0)
    rs(1, 1)
    rs(0, 3)
    loop(4, 10, tap_grads)
    rs(1, 2)
    loop(10, NP, tap_grads)
    rs(1, 3)
    rs(3, 0)
    rs(2, 1)
    dk_acc[...] = jnp.zeros((SPAN, HDIM), F32)
    dv_acc[...] = jnp.zeros((SPAN, HDIM), F32)

    def value_back(i):
        rows = pl.ds(pl.multiple_of(i * BLK, BLK), BLK)
        dv_acc[...] += dot_tn(prob[rows, :], gh[rows, :])

    outs = ((o_gq, 0), (o_gk, 1), (o_gv, 2))

    def d_copy(k, ref, slot):
        peer = mod(f + k, FS)
        return remote(dh.at[slot, at128(peer), :], ref.at[:, at128(f)], d_ss, d_rs.at[slot], (peer, r))

    def attend_back(i):
        i = mod(i + lax.div(f, jnp.int32(2)), SPAN // BLK)
        rows = pl.ds(pl.multiple_of(i * BLK, BLK), BLK)
        grad = gh[rows, :]
        rounded = prob[rows, :]
        weights = rounded.astype(F32)
        grad_probs = dot_nt(grad, qkvh[2])
        row_dot = jnp.sum(weights * grad_probs, axis=1, keepdims=True)
        grad_scores = (weights * (grad_probs - row_dot)).astype(BF16)
        dh[0, rows, :] = (jnp.dot(grad_scores, qkvh[1], preferred_element_type=F32) * INV_ROOT).astype(BF16)
        for half in range(2):
            peer = 2 * i + half

            @pl.when(peer != f)
            def _():
                d_copy(mod(peer - f + FS, FS), o_gq, 0).start()

        dk_acc[...] += dot_tn(grad_scores, qkvh[0, rows, :])

    def tp_copy():
        return remote(tp_s, tp_r, tp_ss, tp_rs, partner)

    def tb_copy(k):
        return remote(tb.at[z], tb.at[z], tb_ss, tb_rs, zline(mod(z + k, NZ)))

    def tc_copy(k):
        return remote(tc_s, tc.at[me], tc_ss, tc_rs, plane(mod(me + k, NP)))

    grad_scale = 1.0 / math.sqrt(SPAN * 32)

    def wgp_copy(half, k):
        peer = mod(me + k, NP)
        return remote(wgp_s.at[half, peer], wgp_r.at[half, k], wgp_ss, wgp_rs.at[half], plane(peer))

    def settle(half):
        for part in (2 * half, 2 * half + 1):
            cols = slice(part * PART, part * PART + PART)
            rs_arrived(0, 3, part)
            rs_arrived(1, 3, part)
            wtmp[:, cols] = chip_sum(z, cols) + rbuf[0, 3, :, cols].astype(F32) + rbuf[1, 3, :, cols].astype(F32)
        for p in range(NP):
            wgp_s[half, p] = wtmp[4 * p : 4 * p + 4, half * 1024 : half * 1024 + 1024].astype(BF16)
        loop(1, NP, lambda k: wgp_copy(half, k).start())

    all_arrived(gh.at[pl.ds(0, 896), :], ga_rs)
    loop(0, SPAN // BLK, value_back)
    dh[2] = dv_acc[...].astype(BF16)
    loop(1, FS, lambda k: d_copy(k, o_gv, 2).start())
    rs(2, 3)
    loop(0, 1, attend_back)
    rs(2, 2)
    loop(1, 2, attend_back)
    rs(3, 1)
    loop(2, 3, attend_back)
    rs(3, 3)
    rs(3, 2)
    all_arrived(ta.at[pl.ds(0, NP - 1)], ta_rs)
    total = tapg[:, at128(me)]
    for k in range(1, NP):
        total = total + ta[k]
    tp_s[...] = total
    tp_copy().start()
    loop(3, 4, attend_back)
    tp_copy().wait_recv()
    tb[z] = (tp_s[...] + tp_r[...]).astype(BF16)
    loop(1, NZ, lambda k: tb_copy(k).start())
    dh[1] = (dk_acc[...] * INV_ROOT).astype(BF16)

    loop(1, FS, lambda k: d_copy(k, o_gk, 1).start())
    for ref, slot in outs:
        ref[:, at128(f)] = dh[slot, at128(f), :]
    settle(0)
    settle(1)
    all_arrived(tb.at[pl.ds(0, NZ - 1)], tb_rs)
    total = tb[0].astype(F32)
    for k in range(1, NZ):
        total = total + tb[k].astype(F32)
    tc_s[...] = (total * grad_scale).astype(BF16)
    loop(1, NP, lambda k: tc_copy(k).start())
    tc[me] = tc_s[...]
    for ref, slot in outs:
        all_arrived(ref.at[:, pl.ds(0, 896)], d_rs.at[slot])
    for half in range(2):
        all_arrived(wgp_r.at[half, pl.ds(0, NP - 1)], wgp_rs.at[half])
        total = wgp_s[half, me].astype(F32)
        for k in range(1, NP):
            total = total + wgp_r[half, k].astype(F32)
        o_wg[:, half * 1024 : half * 1024 + 1024] = total * grad_scale
    all_arrived(tc.at[pl.ds(0, NP - 1)], tc_rs)
    for p in range(NP):
        o_cg[:, p * 128 : p * 128 + 128] = tc[p].astype(F32)[0:KERNEL]

    all_sent(wpl.at[pl.ds(0, NP - 1)], wpl_ss)
    all_sent(qkvh.at[:, pl.ds(0, 896), :], qkv_ss)
    all_sent(wbuf.at[pl.ds(0, 448), :], ag_ss)
    all_sent(wbuf.at[pl.ds(0, 512), :], agp_ss)
    all_sent(attx.at[:, pl.ds(0, 896)], att_ss)
    all_sent(ga_s.at[:, pl.ds(0, 896)], ga_ss)
    all_sent(pbuf, rsp_ss)
    all_sent(wbuf.at[pl.ds(0, 448), :], rs_ss)
    all_sent(dh.at[:, pl.ds(0, 896), :], d_ss)
    all_sent(wgp_s.at[:, pl.ds(0, NP - 1)], wgp_ss)
    all_sent(ta.at[pl.ds(0, NP - 1)], ta_ss)
    all_sent(tb.at[pl.ds(0, NZ - 1)], tb_ss)
    all_sent(tc.at[pl.ds(0, NP - 1)], tc_ss)
    tp_copy().wait_send()

    @pl.when(f > 0)
    def _():
        go_down().wait_send()

    @pl.when(f < FS - 1)
    def _():
        go_up().wait_send()


def put_out(*refs):
    sources, targets, rooms, into, out = refs[:6], refs[6:12], refs[12:18], refs[18], refs[19]
    loads = [pltpu.make_async_copy(sources[i], rooms[i], into.at[i]) for i in range(6)]
    stores = [pltpu.make_async_copy(rooms[i], targets[i], out.at[i]) for i in range(6)]
    for load in loads:
        load.start()
    for load, store in zip(loads, stores):
        load.wait()
        store.start()
    for store in stores:
        store.wait()


def shards(queries, key_rows, value_rows, out_weight, conv_weight, grad_out):
    vmem = pl.BlockSpec(memory_space=pltpu.VMEM)
    hbm = pl.BlockSpec(memory_space=pltpu.HBM)
    anywhere = pl.BlockSpec(memory_space=pl.ANY)
    dma = pltpu.SemaphoreType.DMA
    results = (
        ((ROWS, D), BF16),
        ((ROWS, INNER), BF16),
        ((ROWS, INNER), BF16),
        ((ROWS, INNER), BF16),
        ((4, D), F32),
        ((KERNEL, D), F32),
    )
    shapes = tuple(jax.ShapeDtypeStruct(*result) for result in results)
    found = pl.pallas_call(
        kernel,
        out_shape=shapes,
        in_specs=[hbm] * 6,
        out_specs=(vmem,) * 6,
        scratch_shapes=[
            pltpu.VMEM((3, SPAN, HDIM), BF16),
            pltpu.VMEM((SPAN, SPAN), BF16),
            pltpu.VMEM((SPAN + 2 * HALO, HDIM), BF16),
            pltpu.VMEM((ROWS + 2 * HALO, INNER), BF16),
            pltpu.VMEM((NP, 4, D), BF16),
            pltpu.VMEM((64, D), F32),
            pltpu.VMEM((INNER, D), BF16),
            pltpu.VMEM((INNER, INNER), BF16),
            pltpu.VMEM((ROWS + 2 * HALO, INNER), BF16),
            pltpu.VMEM((INNER, ROWS), BF16),
            pltpu.VMEM((160, D), BF16),
            pltpu.VMEM((KERNEL, D), BF16),
            pltpu.VMEM((KERNEL, 8, D), F32),
            pltpu.VMEM((ROWS + 2 * HALO, COLS), F32),
            pltpu.VMEM((ROWS + 2 * HALO, COLS), F32),
            pltpu.VMEM((ROWS + 2 * HALO, D), F32),
            pltpu.VMEM((160, COLS), F32),
            pltpu.VMEM((ROWS, D), F32),
            pltpu.VMEM((ROWS, COLS), BF16),
            pltpu.VMEM((ROWS, COLS), BF16),
            pltpu.VMEM((INNER, D), BF16),
            pltpu.VMEM((ROWS, INNER), F32),
            pltpu.VMEM((ROWS, INNER), BF16),
            pltpu.VMEM((SPAN, HDIM), BF16),
            pltpu.VMEM((3, SPAN, HDIM), BF16),
            pltpu.VMEM((SPAN, HDIM), F32),
            pltpu.VMEM((SPAN, HDIM), F32),
            pltpu.VMEM((512, D), BF16),
            pltpu.VMEM((2, 4, 64, D), BF16),
            pltpu.VMEM((2, 4, 64, D), BF16),
            pltpu.VMEM((2, NP, 4, 1024), BF16),
            pltpu.VMEM((2, NP, 4, 1024), BF16),
            pltpu.VMEM((32, D), F32),
            pltpu.VMEM((NP, 32, 128), F32),
            pltpu.VMEM((32, 128), F32),
            pltpu.VMEM((32, 128), F32),
            pltpu.VMEM((NZ, 32, 128), BF16),
            pltpu.VMEM((32, 128), BF16),
            pltpu.VMEM((NP, 32, 128), BF16),
            dma((6,)),
            dma, dma((FS,)), dma((2,)),
            dma, dma,
            dma((2,)), dma((2,)),
            dma, dma((2, 4, 4)),
            dma, dma((4,)),
            dma, dma,
            dma, dma,
            dma, dma((4,)),
            dma, dma((2, 4, 4)),
            dma, dma((3,)),
            dma, dma((2,)),
            dma, dma,
            dma, dma,
            dma, dma,
            dma, dma,
        ],
        compiler_params=pltpu.CompilerParams(
            collective_id=0, has_side_effects=True, vmem_limit_bytes=50 * 1024 * 1024
        ),
    )(
        *(
            pltpu.with_memory_space_constraint(given, pltpu.HBM)
            for given in (queries[0], key_rows[0], value_rows[0], out_weight, conv_weight, grad_out[0])
        )
    )
    block_out, grad_queries, grad_keys, grad_values, weight_grad, conv_grad = pl.pallas_call(
        put_out,
        out_shape=shapes,
        in_specs=[anywhere] * 6,
        out_specs=(hbm,) * 6,
        scratch_shapes=[pltpu.VMEM(*result) for result in results] + [dma((6,)), dma((6,))],
        compiler_params=pltpu.CompilerParams(vmem_limit_bytes=8 * 1024 * 1024),
    )(*found)
    return (block_out[None], grad_queries[None], grad_keys[None], grad_values[None], weight_grad, conv_grad)


def solution(mesh):
    return jax.shard_map(
        shards,
        mesh=mesh,
        in_specs=(
            P("frame", "fsdp", None),
            P("frame", "fsdp", None),
            P("frame", "fsdp", None),
            P(("fsdp", "frame"), None),
            P(),
            P("frame", "fsdp", None),
        ),
        out_specs=(
            P("frame", "fsdp", None),
            P("frame", "fsdp", None),
            P("frame", "fsdp", None),
            P("frame", "fsdp", None),
            P(("fsdp", "frame"), None),
            P(),
        ),
        check_vma=False,
    )
```

```python
import math

import jax
import jax.numpy as jnp
from jax import lax
from jax.experimental import pallas as pl
from jax.experimental.pallas import tpu as pltpu
from jax.sharding import PartitionSpec as P

MESH = pl.DeviceIdType.MESH
HDIM = 128
KERNEL = 31
ROWS = 128
INNER = 1024
D = 2048
SPAN = 1024
FS = 8
NZ = 8
NP = 16
HALO = 32
COLS = 256
PART = 512
BLK = 256
INV_ROOT = 1.0 / math.sqrt(HDIM)
EXP_SCALE = INV_ROOT * math.log2(math.e)
F32 = jnp.float32
BF16 = jnp.bfloat16


def mod(a, n):
    return lax.rem(a, jnp.int32(n))


def remote(src, dst, send, recv, device):
    return pltpu.make_async_remote_copy(
        src_ref=src, dst_ref=dst, send_sem=send, recv_sem=recv, device_id=device, device_id_type=MESH
    )


def loop(lower, upper, body):
    def step(i, carry):
        body(i)
        return carry

    lax.fori_loop(lower, upper, step, 0)


def at128(i):
    return pl.ds(pl.multiple_of(i * 128, 128), 128)


def at64(i):
    return pl.ds(pl.multiple_of(i * 64, 64), 64)


def dot_nt(a, b):
    return lax.dot_general(a, b, (((1,), (1,)), ((), ())), preferred_element_type=F32)


def dot_tn(a, b):
    return lax.dot_general(a, b, (((0,), (0,)), ((), ())), preferred_element_type=F32)


def kernel(
    q_ref, k_ref, v_ref, w_ref, taps_ref, go_ref,
    o_block, o_gq, o_gk, o_gv, o_wg, o_cg,
    qkvh, prob, ohp, attx, wpl, wtmp, wbuf, perm, attp, attt, gox, tapv, tapb, proj_s, next_s, proj_all, gc_s, gc_all, gp_s, last_s, wgs,
    ga_acc, ga_s, gh, dh, dk_acc, dv_acc, pbuf, sbuf, rbuf, wgp_s, wgp_r, pw_s, pw_r, pz_s, pz_r,
    tapg, ta, tp_s, tp_r, tb, tc_s, tc,
    own_s, qkv_ss, q_rs, kv_rs, wpl_ss, wpl_rs, go_ss, go_rs, ag_ss, ag_rs, agp_ss, agp_rs, att_ss, att_rs,
    ga_ss, ga_rs, rsp_ss, rsp_rs, rs_ss, rs_rs, d_ss, d_rs, wgp_ss, wgp_rs, pw_ss, pw_rs, pz_ss, pz_rs,
    ta_ss, ta_rs, tp_ss, tp_rs, tb_ss, tb_rs, tc_ss, tc_rs,
):
    f = lax.axis_index("fsdp").astype(jnp.int32)
    r = lax.axis_index("frame").astype(jnp.int32)
    ylo = lax.div(r, jnp.int32(16))
    z = mod(lax.div(r, jnp.int32(2)), NZ)
    core = mod(r, 2)
    me = f * 2 + ylo

    def plane(p):
        return (lax.div(p, jnp.int32(2)), mod(p, 2) * 16 + z * 2 + core)

    def zline(other):
        return (f, ylo * 16 + other * 2 + core)

    partner = (f, ylo * 16 + z * 2 + 1 - core)

    def all_arrived(ref, sem):
        remote(ref, ref, sem, sem, partner).wait_recv()

    def all_sent(ref, sem):
        remote(ref, ref, sem, sem, partner).wait_send()

    heads = ((q_ref, 0), (k_ref, 1), (v_ref, 2))

    def own_copies():
        for source, slot in heads:
            yield pltpu.make_async_copy(source.at[:, at128(f)], qkvh.at[slot, at128(f), :], own_s.at[slot])
        yield pltpu.make_async_copy(go_ref, gox.at[pl.ds(16, ROWS), :], own_s.at[3])
        yield pltpu.make_async_copy(w_ref, wpl.at[me], own_s.at[4])
        yield pltpu.make_async_copy(taps_ref, tapv, own_s.at[5])

    barrier = pltpu.get_barrier_semaphore()

    def greet_plane(k):
        pl.semaphore_signal(barrier, inc=1, device_id=plane(mod(me + k, NP)), device_id_type=MESH)

    def greet_z(k):
        pl.semaphore_signal(barrier, inc=1, device_id=zline(mod(z + k, NZ)), device_id_type=MESH)

    loop(1, NP, greet_plane)
    loop(1, NZ, greet_z)
    pl.semaphore_signal(barrier, inc=1, device_id=partner, device_id_type=MESH)
    for copy in own_copies():
        copy.start()

    @pl.when(f == 0)
    def _():
        gox[0:16, :] = jnp.zeros((16, D), BF16)

    @pl.when(f == FS - 1)
    def _():
        gox[144:160, :] = jnp.zeros((16, D), BF16)

    ohp[0:HALO, :] = jnp.zeros((HALO, HDIM), BF16)
    ohp[HALO + SPAN : HALO + SPAN + HALO, :] = jnp.zeros((HALO, HDIM), BF16)

    def perm_rows(b):
        row = lax.broadcasted_iota(jnp.int32, (128, INNER), 0) + b * 128
        col = lax.broadcasted_iota(jnp.int32, (128, INNER), 1)
        at = ((col >> 2) & 15) * 64 + ((col >> 6) & 7) * 8 + (col >> 9) * 4 + (col & 3)
        perm[at128(b), :] = jnp.where(row == at, 1.0, 0.0).astype(BF16)

    loop(0, 8, perm_rows)
    for copy in own_copies():
        copy.wait()
    taps = tapv[...].astype(F32)
    for j in range(KERNEL):
        tapb[j] = jnp.broadcast_to(taps[j : j + 1, :], (8, D))
    pl.semaphore_wait(barrier, NP - 1 + NZ - 1 + 1)

    def wpl_copy(k):
        return remote(w_ref, wpl.at[me], wpl_ss, wpl_rs, plane(mod(me + k, NP)))

    loop(1, NP, lambda k: wpl_copy(k).start())

    def qkv_copy(k, source, slot):
        peer = mod(f + k, FS)
        arrival = q_rs.at[k] if slot == 0 else kv_rs.at[slot - 1]
        return remote(source.at[:, at128(peer)], qkvh.at[slot, at128(f), :], qkv_ss, arrival, (peer, r))

    def go_down():
        return remote(go_ref.at[pl.ds(0, 16), :], gox.at[pl.ds(144, 16), :], go_ss.at[0], go_rs.at[0], (f - 1, r))

    def go_up():
        return remote(go_ref.at[pl.ds(112, 16), :], gox.at[pl.ds(0, 16), :], go_ss.at[1], go_rs.at[1], (f + 1, r))

    loop(1, FS, lambda k: qkv_copy(k, k_ref, 1).start())
    all_arrived(wpl.at[pl.ds(0, NP - 1)], wpl_rs)
    for p in range(NP):
        wtmp[4 * p : 4 * p + 4, :] = wpl[p].astype(F32)

    def wblock(c, zz):
        return pl.ds(pl.multiple_of(c * 512 + zz * 64, 64), 64)

    wbuf[wblock(core, z), :] = wtmp[...].astype(BF16)

    up, down = zline(mod(z + 1, NZ)), zline(mod(z + NZ - 1, NZ))

    def ag_part(part):
        return pl.ds(part * PART, PART)

    def ag_copy(way, s, part):
        block = mod(z - s + NZ, NZ) if way == 0 else mod(z + s, NZ)
        view = wbuf.at[wblock(core, block), ag_part(part)]
        return remote(view, view, ag_ss, ag_rs.at[way, s, part], up if way == 0 else down)

    def ag_arrived(way, s, part):
        block = mod(z - 1 - s + NZ, NZ) if way == 0 else mod(z + 1 + s, NZ)
        view = wbuf.at[wblock(core, block), ag_part(part)]
        remote(view, view, ag_ss, ag_rs.at[way, s, part], down if way == 0 else up).wait_recv()

    def agp_copy(k, part):
        view = wbuf.at[wblock(core, mod(z + k, NZ)), ag_part(part)]
        return remote(view, view, agp_ss, agp_rs.at[part], partner)

    def goes_far(way, s, part):
        return s < 3 or part % 2 == way

    def ag_first(*parts):
        for part in parts:
            for way in range(2):
                ag_copy(way, 0, part).start()
        for part in parts:
            agp_copy(0, part).start()

    def ag_turn(s, *parts):
        for part in parts:
            for way in range(2):
                if goes_far(way, s, part):
                    ag_arrived(way, s, part)
                    if s < 3 and goes_far(way, s + 1, part):
                        ag_copy(way, s + 1, part).start()
            if s < 3:
                agp_copy(NZ - 1 - s, part).start()
                agp_copy(1 + s, part).start()
            else:
                agp_copy(4, part).start()

    def agp_arrived(part):
        all_arrived(wbuf.at[pl.ds(0, 512), ag_part(part)], agp_rs.at[part])

    ag_first(0, 1, 2)
    loop(1, FS, lambda k: qkv_copy(k, v_ref, 2).start())
    loop(1, FS, lambda k: qkv_copy(k, q_ref, 0).start())

    @pl.when(f > 0)
    def _():
        go_down().start()

    @pl.when(f < FS - 1)
    def _():
        go_up().start()

    ag_turn(0, 0, 1, 2)

    def query_arrived(source):
        arrival = q_rs.at[mod(f - source + FS, FS)]
        remote(q_ref.at[:, at128(source)], qkvh.at[0, at128(source), :], qkv_ss, arrival, (source, r)).wait_recv()

    for slot in (1, 2):
        all_arrived(qkvh.at[slot, pl.ds(0, 896), :], kv_rs.at[slot - 1])

    def ext(i):
        return pl.ds(pl.multiple_of(i * ROWS, ROWS), ROWS + 2 * HALO)

    def att_copy(k):
        peer = mod(f + k, FS)
        return remote(ohp.at[ext(peer), :], attx.at[:, at128(f)], att_ss, att_rs, (peer, r))

    first = lax.div(f, jnp.int32(2))

    def att_send(i):
        for half in range(2):
            peer = mod(2 * (first + i) - 1 + half + FS, FS)

            @pl.when(peer != f)
            def _():
                att_copy(mod(peer - f + FS, FS)).start()

    def attend(i):
        block = mod(first + i, SPAN // BLK)
        for half in range(2):
            source = 2 * block + half

            @pl.when(source != f)
            def _():
                query_arrived(source)

        rows = pl.ds(pl.multiple_of(block * BLK, BLK), BLK)
        scores = dot_nt(qkvh[0, rows, :], qkvh[1])
        exponent = jnp.exp2((scores - jnp.max(scores, axis=1, keepdims=True)) * EXP_SCALE)
        rounded = (exponent * (1.0 / jnp.sum(exponent, axis=1, keepdims=True))).astype(BF16)
        prob[rows, :] = rounded
        attended = jnp.dot(rounded, qkvh[2], preferred_element_type=F32)
        ohp[pl.ds(pl.multiple_of(block * BLK + HALO, HALO), BLK), :] = attended.astype(BF16)

        @pl.when(i > 0)
        def _():
            att_send(i)

        for part in range(3):

            @pl.when(i == part)
            def _():
                ag_turn(1, part)

    loop(0, SPAN // BLK, attend)
    att_send(SPAN // BLK)
    attx[:, at128(f)] = ohp[ext(f), :]
    ag_turn(2, 0, 1, 2)
    ag_first(3)
    ag_turn(3, 0, 1, 2)
    ag_turn(0, 3)

    @pl.when(f < FS - 1)
    def _():
        remote(go_ref.at[pl.ds(0, 16), :], gox.at[pl.ds(144, 16), :], go_ss.at[0], go_rs.at[0], (f + 1, r)).wait_recv()

    @pl.when(f > 0)
    def _():
        remote(go_ref.at[pl.ds(112, 16), :], gox.at[pl.ds(0, 16), :], go_ss.at[1], go_rs.at[1], (f - 1, r)).wait_recv()

    all_arrived(attx.at[:, pl.ds(0, 896)], att_rs)
    attp[...] = jnp.dot(attx[...], perm[...], preferred_element_type=F32).astype(BF16)
    attt[...] = attp[HALO : HALO + ROWS, :].T
    agp_arrived(0)
    grad_scale = 1.0 / math.sqrt(SPAN * 32)
    ga_acc[...] = jnp.zeros((ROWS, INNER), F32)
    tapg[KERNEL : KERNEL + 1, :] = jnp.zeros((1, D), F32)

    def rsp_copy(part):
        cols = pl.ds(pl.multiple_of(part * PART, PART), PART)
        rows = pl.ds(pl.multiple_of((1 - core) * 512, 512), 512)
        return remote(wgs.at[rows, cols], pbuf.at[:, cols], rsp_ss, rsp_rs.at[part], partner)

    def rsp_arrived(part):
        cols = pl.ds(part * PART, PART)
        rows = pl.ds(pl.multiple_of(core * 512, 512), 512)
        remote(wgs.at[rows, cols], pbuf.at[:, cols], rsp_ss, rsp_rs.at[part], partner).wait_recv()

    def ta_copy(k):
        peer = mod(me + k, NP)
        return remote(tapg.at[:, at128(peer)], ta.at[k], ta_ss, ta_rs, plane(peer))

    def takes_part(way, s, part):
        return s > 0 or (part % 2 == 1) == (way == 0)

    def rs_copy(way, s, part):
        view = (way, s, slice(None), pl.ds(part * PART, PART))
        return remote(
            sbuf.at[view], rbuf.at[view], rs_ss, rs_rs.at[way, s, part], up if way == 0 else down
        )

    def rs_arrived(way, s, part):
        view = (way, s, slice(None), pl.ds(part * PART, PART))
        remote(
            sbuf.at[view], rbuf.at[view], rs_ss, rs_rs.at[way, s, part], down if way == 0 else up
        ).wait_recv()

    def chip_sum(block, cols):
        return wgs[wblock(core, block), cols].astype(F32) + pbuf[at64(block), cols].astype(F32)

    def rs(s, part):
        cols = slice(part * PART, part * PART + PART)
        if s == 0:
            rsp_arrived(part)
        for way in range(2):
            if not takes_part(way, s, part):
                continue
            block = mod(z + 4 - s, NZ) if way == 0 else mod(z + 4 + s, NZ)
            value = chip_sum(block, cols)
            if s > 0 and takes_part(way, s - 1, part):
                rs_arrived(way, s - 1, part)
                value = value + rbuf[way, s - 1, :, cols].astype(F32)
            sbuf[way, s, :, cols] = value.astype(BF16)
            rs_copy(way, s, part).start()

    def pw_copy(part, k):
        peer = mod(me + k, NP)
        return remote(pw_s.at[part, peer], pw_r.at[part, k], pw_ss, pw_rs.at[part], plane(peer))

    def pz_copy(part, k):
        other = mod(z + k, NZ)
        return remote(pz_s.at[part, other], pz_r.at[part, k], pz_ss, pz_rs.at[part], zline(other))

    def early_give(part):
        rsp_arrived(part)

        def pack(zz):
            wtmp[:, 0:PART] = chip_sum(zz, slice(part * PART, part * PART + PART))
            for p in range(NP):
                pw_s[part, p, zz] = wtmp[4 * p : 4 * p + 4, 0:PART].astype(BF16)

        loop(0, NZ, pack)
        loop(1, NP, lambda k: pw_copy(part, k).start())

    def early_sum(part):
        all_arrived(pw_r.at[part, pl.ds(0, NP - 1)], pw_rs.at[part])

        def add(zz):
            total = pw_s[part, me, zz].astype(F32)
            for k in range(1, NP):
                total = total + pw_r[part, k, zz].astype(F32)
            pz_s[part, zz] = total.astype(BF16)

        loop(0, NZ, add)
        loop(1, NZ, lambda k: pz_copy(part, k).start())

    def early_end(part):
        all_arrived(pz_r.at[part, pl.ds(0, NZ - 1)], pz_rs.at[part])
        total = pz_s[part, z].astype(F32)
        for k in range(1, NZ):
            total = total + pz_r[part, k].astype(F32)
        o_wg[:, part * PART : part * PART + PART] = total * grad_scale

    def at_cols(c):
        return pl.ds(pl.multiple_of(c * COLS, COLS), COLS)

    def project(c):
        next_s[...] = jnp.dot(attp[...], wbuf[:, at_cols(c)], preferred_element_type=F32).astype(BF16).astype(F32)

    def pull_back(c):
        gp = last_s[...]
        wgs[:, at_cols(c)] = jnp.dot(attt[...], gp, preferred_element_type=F32).astype(BF16)
        ga_acc[...] += dot_nt(gp, wbuf[:, at_cols(c)])

    events = {
        0: ((ag_turn, 1, 3), (agp_arrived, 1)),
        2: ((ag_turn, 2, 3), (agp_arrived, 2)),
        3: ((early_give, 0),),
        4: ((ag_turn, 3, 3), (agp_arrived, 3)),
        5: ((early_give, 1),),
        7: ((rs, 0, 2),),
    }

    def tap_grads(tile):
        here = at128(tile)
        gc_own = gc_all[:, here].reshape(16, 8, 128)
        for shift in range(8):
            moved = proj_all[shift : shift + 184, here]
            for j in range(KERNEL):
                if (17 + j) % 8 == shift:
                    start = 17 + j - shift
                    partial = jnp.sum(gc_own * moved[start : start + 128].reshape(16, 8, 128), axis=0)
                    tapg[j : j + 1, here] = jnp.sum(partial, axis=0, keepdims=True)

        @pl.when(tile != me)
        def _():
            ta_copy(mod(tile - me + NP, NP)).start()

    def columns(c):
        project(jnp.minimum(c + 1, D // COLS - 1))
        pull_back(jnp.maximum(c - 1, 0))
        for lane in range(COLS // 128):
            here = pl.ds(pl.multiple_of(c * COLS + lane * 128, 128), 128)
            local = slice(lane * 128, lane * 128 + 128)
            conv = jnp.zeros((20, 8, 128), F32)
            for shift in range(8):
                moved = proj_s[shift : shift + 184, local]
                for j in range(KERNEL):
                    if (1 + j) % 8 == shift:
                        start = 1 + j - shift
                        conv = conv + tapb[j, :, here][None] * moved[start : start + 160].reshape(20, 8, 128)
            conv = conv.reshape(160, 128)
            sig = jax.nn.sigmoid(conv)
            upstream = gox[:, here].astype(F32)
            o_block[:, here] = (proj_s[32:160, local] + conv[16:144] * sig[16:144]).astype(BF16)
            grad_conv = (upstream * sig * (1.0 + conv * (1.0 - sig))).astype(BF16).astype(F32)
            gc_s[:, local] = grad_conv
            gc_all[:, here] = grad_conv[16:144]
            total = gox[16:144, here].astype(F32).reshape(16, 8, 128)
            for shift in range(8):
                moved = gc_s[shift : shift + 152, local]
                for j in range(KERNEL):
                    if (31 - j) % 8 == shift:
                        start = 31 - j - shift
                        total = total + tapb[j, :, here][None] * moved[start : start + 128].reshape(16, 8, 128)
            gp_s[:, local] = total.reshape(128, 128).astype(BF16)
        proj_all[:, at_cols(c)] = proj_s[...]
        proj_s[...] = next_s[...]
        last_s[...] = gp_s[...]

        @pl.when((c > 0) & (mod(c, 2) == 0))
        def _():
            rsp_copy(lax.div(c, jnp.int32(2)) - 1).start()

        for at, calls in events.items():

            @pl.when(c == at)
            def _():
                for call, *given in calls:
                    call(*given)

    project(0)
    proj_s[...] = next_s[...]
    last_s[...] = jnp.zeros((ROWS, COLS), BF16)
    loop(0, D // COLS, columns)
    pull_back(D // COLS - 1)
    rsp_copy(3).start()
    ga_s[...] = dot_nt(ga_acc[...].astype(BF16), perm[...]).astype(BF16)

    def ga_copy(k):
        peer = mod(f + k, FS)
        return remote(ga_s.at[:, at128(peer)], gh.at[at128(f), :], ga_ss, ga_rs, (peer, r))

    loop(1, FS, lambda k: ga_copy(k).start())

    gh[at128(f), :] = ga_s[:, at128(f)]
    loop(0, 4, tap_grads)
    rs(0, 3)
    rs(1, 2)
    loop(4, 10, tap_grads)
    early_sum(0)
    loop(10, NP, tap_grads)
    rs(1, 3)
    rs(2, 2)
    early_sum(1)
    dk_acc[...] = jnp.zeros((SPAN, HDIM), F32)
    dv_acc[...] = jnp.zeros((SPAN, HDIM), F32)

    def value_back(i):
        rows = pl.ds(pl.multiple_of(i * BLK, BLK), BLK)
        dv_acc[...] += dot_tn(prob[rows, :], gh[rows, :])

    outs = ((o_gq, 0), (o_gk, 1), (o_gv, 2))

    def d_copy(k, ref, slot):
        peer = mod(f + k, FS)
        return remote(dh.at[slot, at128(peer), :], ref.at[:, at128(f)], d_ss, d_rs.at[slot], (peer, r))

    def attend_back(i):
        i = mod(i + lax.div(f, jnp.int32(2)), SPAN // BLK)
        rows = pl.ds(pl.multiple_of(i * BLK, BLK), BLK)
        grad = gh[rows, :]
        rounded = prob[rows, :]
        weights = rounded.astype(F32)
        grad_probs = dot_nt(grad, qkvh[2])
        row_dot = jnp.sum(weights * grad_probs, axis=1, keepdims=True)
        grad_scores = (weights * (grad_probs - row_dot)).astype(BF16)
        dh[0, rows, :] = (jnp.dot(grad_scores, qkvh[1], preferred_element_type=F32) * INV_ROOT).astype(BF16)
        for half in range(2):
            peer = 2 * i + half

            @pl.when(peer != f)
            def _():
                d_copy(mod(peer - f + FS, FS), o_gq, 0).start()

        dk_acc[...] += dot_tn(grad_scores, qkvh[0, rows, :])

    def tp_copy():
        return remote(tp_s, tp_r, tp_ss, tp_rs, partner)

    def tb_copy(k):
        return remote(tb.at[z], tb.at[z], tb_ss, tb_rs, zline(mod(z + k, NZ)))

    def tc_copy(k):
        return remote(tc_s, tc.at[me], tc_ss, tc_rs, plane(mod(me + k, NP)))


    def wgp_copy(half, k):
        peer = mod(me + k, NP)
        return remote(wgp_s.at[half, peer], wgp_r.at[half, k], wgp_ss, wgp_rs.at[half], plane(peer))

    def settle(half):
        for part in (2 * half, 2 * half + 1):
            cols = slice(part * PART, part * PART + PART)
            rs_arrived(0, 3, part)
            rs_arrived(1, 3, part)
            wtmp[:, cols] = chip_sum(z, cols) + rbuf[0, 3, :, cols].astype(F32) + rbuf[1, 3, :, cols].astype(F32)
        for p in range(NP):
            wgp_s[half, p] = wtmp[4 * p : 4 * p + 4, half * 1024 : half * 1024 + 1024].astype(BF16)
        loop(1, NP, lambda k: wgp_copy(half, k).start())

    all_arrived(gh.at[pl.ds(0, 896), :], ga_rs)
    loop(0, SPAN // BLK, value_back)
    dh[2] = dv_acc[...].astype(BF16)
    loop(1, FS, lambda k: d_copy(k, o_gv, 2).start())
    loop(0, 1, attend_back)
    rs(2, 3)
    rs(3, 2)
    all_arrived(ta.at[pl.ds(0, NP - 1)], ta_rs)
    total = tapg[:, at128(me)]
    for k in range(1, NP):
        total = total + ta[k]
    tp_s[...] = total
    tp_copy().start()
    loop(1, 2, attend_back)
    tp_copy().wait_recv()
    tb[z] = (tp_s[...] + tp_r[...]).astype(BF16)
    loop(1, NZ, lambda k: tb_copy(k).start())
    loop(2, 4, attend_back)
    dh[1] = (dk_acc[...] * INV_ROOT).astype(BF16)

    loop(1, FS, lambda k: d_copy(k, o_gk, 1).start())
    for ref, slot in outs:
        ref[:, at128(f)] = dh[slot, at128(f), :]
    rs(3, 3)
    early_end(0)
    early_end(1)
    settle(1)
    all_arrived(tb.at[pl.ds(0, NZ - 1)], tb_rs)
    total = tb[0].astype(F32)
    for k in range(1, NZ):
        total = total + tb[k].astype(F32)
    tc_s[...] = (total * grad_scale).astype(BF16)
    loop(1, NP, lambda k: tc_copy(k).start())
    tc[me] = tc_s[...]
    for ref, slot in outs:
        all_arrived(ref.at[:, pl.ds(0, 896)], d_rs.at[slot])
    all_arrived(wgp_r.at[1, pl.ds(0, NP - 1)], wgp_rs.at[1])
    total = wgp_s[1, me].astype(F32)
    for k in range(1, NP):
        total = total + wgp_r[1, k].astype(F32)
    o_wg[:, 1024:D] = total * grad_scale
    all_arrived(tc.at[pl.ds(0, NP - 1)], tc_rs)
    for p in range(NP):
        o_cg[:, p * 128 : p * 128 + 128] = tc[p].astype(F32)[0:KERNEL]

    all_sent(wpl.at[pl.ds(0, NP - 1)], wpl_ss)
    all_sent(qkvh.at[:, pl.ds(0, 896), :], qkv_ss)
    all_sent(wbuf.at[pl.ds(0, 448), :], ag_ss)
    all_sent(wbuf.at[pl.ds(0, 512), :], agp_ss)
    all_sent(attx.at[:, pl.ds(0, 896)], att_ss)
    all_sent(ga_s.at[:, pl.ds(0, 896)], ga_ss)
    all_sent(pbuf, rsp_ss)
    all_sent(wbuf.at[pl.ds(0, 224), :], rs_ss)
    all_sent(pw_s.at[:, pl.ds(0, NP - 1)], pw_ss)
    all_sent(pz_s.at[:, pl.ds(0, NZ - 1)], pz_ss)
    all_sent(dh.at[:, pl.ds(0, 896), :], d_ss)
    all_sent(wgp_s.at[1, pl.ds(0, NP - 1)], wgp_ss)
    all_sent(ta.at[pl.ds(0, NP - 1)], ta_ss)
    all_sent(tb.at[pl.ds(0, NZ - 1)], tb_ss)
    all_sent(tc.at[pl.ds(0, NP - 1)], tc_ss)
    tp_copy().wait_send()

    @pl.when(f > 0)
    def _():
        go_down().wait_send()

    @pl.when(f < FS - 1)
    def _():
        go_up().wait_send()


def put_out(*refs):
    sources, targets, rooms, into, out = refs[:6], refs[6:12], refs[12:18], refs[18], refs[19]
    loads = [pltpu.make_async_copy(sources[i], rooms[i], into.at[i]) for i in range(6)]
    stores = [pltpu.make_async_copy(rooms[i], targets[i], out.at[i]) for i in range(6)]
    for load in loads:
        load.start()
    for load, store in zip(loads, stores):
        load.wait()
        store.start()
    for store in stores:
        store.wait()


def shards(queries, key_rows, value_rows, out_weight, conv_weight, grad_out):
    vmem = pl.BlockSpec(memory_space=pltpu.VMEM)
    hbm = pl.BlockSpec(memory_space=pltpu.HBM)
    anywhere = pl.BlockSpec(memory_space=pl.ANY)
    dma = pltpu.SemaphoreType.DMA
    results = (
        ((ROWS, D), BF16),
        ((ROWS, INNER), BF16),
        ((ROWS, INNER), BF16),
        ((ROWS, INNER), BF16),
        ((4, D), F32),
        ((KERNEL, D), F32),
    )
    shapes = tuple(jax.ShapeDtypeStruct(*result) for result in results)
    found = pl.pallas_call(
        kernel,
        out_shape=shapes,
        in_specs=[hbm] * 6,
        out_specs=(vmem,) * 6,
        scratch_shapes=[
            pltpu.VMEM((3, SPAN, HDIM), BF16),
            pltpu.VMEM((SPAN, SPAN), BF16),
            pltpu.VMEM((SPAN + 2 * HALO, HDIM), BF16),
            pltpu.VMEM((ROWS + 2 * HALO, INNER), BF16),
            pltpu.VMEM((NP, 4, D), BF16),
            pltpu.VMEM((64, D), F32),
            pltpu.VMEM((INNER, D), BF16),
            pltpu.VMEM((INNER, INNER), BF16),
            pltpu.VMEM((ROWS + 2 * HALO, INNER), BF16),
            pltpu.VMEM((INNER, ROWS), BF16),
            pltpu.VMEM((160, D), BF16),
            pltpu.VMEM((KERNEL, D), BF16),
            pltpu.VMEM((KERNEL, 8, D), F32),
            pltpu.VMEM((ROWS + 2 * HALO, COLS), F32),
            pltpu.VMEM((ROWS + 2 * HALO, COLS), F32),
            pltpu.VMEM((ROWS + 2 * HALO, D), F32),
            pltpu.VMEM((160, COLS), F32),
            pltpu.VMEM((ROWS, D), F32),
            pltpu.VMEM((ROWS, COLS), BF16),
            pltpu.VMEM((ROWS, COLS), BF16),
            pltpu.VMEM((INNER, D), BF16),
            pltpu.VMEM((ROWS, INNER), F32),
            pltpu.VMEM((ROWS, INNER), BF16),
            pltpu.VMEM((SPAN, HDIM), BF16),
            pltpu.VMEM((3, SPAN, HDIM), BF16),
            pltpu.VMEM((SPAN, HDIM), F32),
            pltpu.VMEM((SPAN, HDIM), F32),
            pltpu.VMEM((512, D), BF16),
            pltpu.VMEM((2, 4, 64, D), BF16),
            pltpu.VMEM((2, 4, 64, D), BF16),
            pltpu.VMEM((2, NP, 4, 1024), BF16),
            pltpu.VMEM((2, NP, 4, 1024), BF16),
            pltpu.VMEM((2, NP, NZ, 4, PART), BF16),
            pltpu.VMEM((2, NP, NZ, 4, PART), BF16),
            pltpu.VMEM((2, NZ, 4, PART), BF16),
            pltpu.VMEM((2, NZ, 4, PART), BF16),
            pltpu.VMEM((32, D), F32),
            pltpu.VMEM((NP, 32, 128), F32),
            pltpu.VMEM((32, 128), F32),
            pltpu.VMEM((32, 128), F32),
            pltpu.VMEM((NZ, 32, 128), BF16),
            pltpu.VMEM((32, 128), BF16),
            pltpu.VMEM((NP, 32, 128), BF16),
            dma((6,)),
            dma, dma((FS,)), dma((2,)),
            dma, dma,
            dma((2,)), dma((2,)),
            dma, dma((2, 4, 4)),
            dma, dma((4,)),
            dma, dma,
            dma, dma,
            dma, dma((4,)),
            dma, dma((2, 4, 4)),
            dma, dma((3,)),
            dma, dma((2,)),
            dma, dma((2,)),
            dma, dma((2,)),
            dma, dma,
            dma, dma,
            dma, dma,
            dma, dma,
        ],
        compiler_params=pltpu.CompilerParams(
            collective_id=0, has_side_effects=True, vmem_limit_bytes=50 * 1024 * 1024
        ),
    )(
        *(
            pltpu.with_memory_space_constraint(given, pltpu.HBM)
            for given in (queries[0], key_rows[0], value_rows[0], out_weight, conv_weight, grad_out[0])
        )
    )
    block_out, grad_queries, grad_keys, grad_values, weight_grad, conv_grad = pl.pallas_call(
        put_out,
        out_shape=shapes,
        in_specs=[anywhere] * 6,
        out_specs=(hbm,) * 6,
        scratch_shapes=[pltpu.VMEM(*result) for result in results] + [dma((6,)), dma((6,))],
        compiler_params=pltpu.CompilerParams(vmem_limit_bytes=8 * 1024 * 1024),
    )(*found)
    return (block_out[None], grad_queries[None], grad_keys[None], grad_values[None], weight_grad, conv_grad)


def solution(mesh):
    return jax.shard_map(
        shards,
        mesh=mesh,
        in_specs=(
            P("frame", "fsdp", None),
            P("frame", "fsdp", None),
            P("frame", "fsdp", None),
            P(("fsdp", "frame"), None),
            P(),
            P("frame", "fsdp", None),
        ),
        out_specs=(
            P("frame", "fsdp", None),
            P("frame", "fsdp", None),
            P("frame", "fsdp", None),
            P("frame", "fsdp", None),
            P(("fsdp", "frame"), None),
            P(),
        ),
        check_vma=False,
    )
```

```python
import math

import jax
import jax.numpy as jnp
from jax import lax
from jax.experimental import pallas as pl
from jax.experimental.pallas import tpu as pltpu
from jax.sharding import PartitionSpec as P

MESH = pl.DeviceIdType.MESH
HDIM = 128
KERNEL = 31
ROWS = 128
INNER = 1024
D = 2048
SPAN = 1024
FS = 8
NZ = 8
NP = 16
HALO = 32
COLS = 256
PART = 512
BLK = 256
INV_ROOT = 1.0 / math.sqrt(HDIM)
EXP_SCALE = INV_ROOT * math.log2(math.e)
F32 = jnp.float32
BF16 = jnp.bfloat16


def mod(a, n):
    return lax.rem(a, jnp.int32(n))


def remote(src, dst, send, recv, device):
    return pltpu.make_async_remote_copy(
        src_ref=src, dst_ref=dst, send_sem=send, recv_sem=recv, device_id=device, device_id_type=MESH
    )


def loop(lower, upper, body):
    def step(i, carry):
        body(i)
        return carry

    lax.fori_loop(lower, upper, step, 0)


def at128(i):
    return pl.ds(pl.multiple_of(i * 128, 128), 128)


def at64(i):
    return pl.ds(pl.multiple_of(i * 64, 64), 64)


def dot_nt(a, b):
    return lax.dot_general(a, b, (((1,), (1,)), ((), ())), preferred_element_type=F32)


def dot_tn(a, b):
    return lax.dot_general(a, b, (((0,), (0,)), ((), ())), preferred_element_type=F32)


def kernel(
    q_ref, k_ref, v_ref, w_ref, taps_ref, go_ref,
    o_block, o_gq, o_gk, o_gv, o_wg, o_cg,
    qkvh, prob, ohp, attx, wpl, wtmp, wbuf, perm, attp, attt, gox, tapv, tapb, proj_s, next_s, proj_all, gc_s, gc_all, gp_s, last_s, wgs,
    ga_acc, ga_s, gh, dh, dk_acc, dv_acc, pbuf, sbuf, rbuf, wgp_s, wgp_r, pw_s, pw_r, pz_s, pz_r,
    tapg, ta, tp_s, tp_r, tb, tc_s, tc,
    own_s, qkv_ss, q_rs, kv_rs, wpl_ss, wpl_rs, go_ss, go_rs, ag_ss, ag_rs, agp_ss, agp_rs, att_ss, att_rs,
    ga_ss, ga_rs, rsp_ss, rsp_rs, rs_ss, rs_rs, d_ss, d_rs, wgp_ss, wgp_rs, pw_ss, pw_rs, pz_ss, pz_rs,
    ta_ss, ta_rs, tp_ss, tp_rs, tb_ss, tb_rs, tc_ss, tc_rs,
):
    f = lax.axis_index("fsdp").astype(jnp.int32)
    r = lax.axis_index("frame").astype(jnp.int32)
    ylo = lax.div(r, jnp.int32(16))
    z = mod(lax.div(r, jnp.int32(2)), NZ)
    core = mod(r, 2)
    me = f * 2 + ylo

    def plane(p):
        return (lax.div(p, jnp.int32(2)), mod(p, 2) * 16 + z * 2 + core)

    def zline(other):
        return (f, ylo * 16 + other * 2 + core)

    partner = (f, ylo * 16 + z * 2 + 1 - core)

    def all_arrived(ref, sem):
        remote(ref, ref, sem, sem, partner).wait_recv()

    def all_sent(ref, sem):
        remote(ref, ref, sem, sem, partner).wait_send()

    heads = ((q_ref, 0), (k_ref, 1), (v_ref, 2))

    def own_copies():
        for source, slot in heads:
            yield pltpu.make_async_copy(source.at[:, at128(f)], qkvh.at[slot, at128(f), :], own_s.at[slot])
        yield pltpu.make_async_copy(go_ref, gox.at[pl.ds(16, ROWS), :], own_s.at[3])
        yield pltpu.make_async_copy(w_ref, wpl.at[me], own_s.at[4])
        yield pltpu.make_async_copy(taps_ref, tapv, own_s.at[5])

    barrier = pltpu.get_barrier_semaphore()

    def greet_plane(k):
        pl.semaphore_signal(barrier, inc=1, device_id=plane(mod(me + k, NP)), device_id_type=MESH)

    def greet_z(k):
        pl.semaphore_signal(barrier, inc=1, device_id=zline(mod(z + k, NZ)), device_id_type=MESH)

    loop(1, NP, greet_plane)
    loop(1, NZ, greet_z)
    pl.semaphore_signal(barrier, inc=1, device_id=partner, device_id_type=MESH)
    for copy in own_copies():
        copy.start()

    @pl.when(f == 0)
    def _():
        gox[0:16, :] = jnp.zeros((16, D), BF16)

    @pl.when(f == FS - 1)
    def _():
        gox[144:160, :] = jnp.zeros((16, D), BF16)

    ohp[0:HALO, :] = jnp.zeros((HALO, HDIM), BF16)
    ohp[HALO + SPAN : HALO + SPAN + HALO, :] = jnp.zeros((HALO, HDIM), BF16)

    def perm_rows(b):
        row = lax.broadcasted_iota(jnp.int32, (128, INNER), 0) + b * 128
        col = lax.broadcasted_iota(jnp.int32, (128, INNER), 1)
        at = ((col >> 2) & 15) * 64 + ((col >> 6) & 7) * 8 + (col >> 9) * 4 + (col & 3)
        perm[at128(b), :] = jnp.where(row == at, 1.0, 0.0).astype(BF16)

    loop(0, 8, perm_rows)
    for copy in own_copies():
        copy.wait()
    taps = tapv[...].astype(F32)
    for j in range(KERNEL):
        tapb[j] = jnp.broadcast_to(taps[j : j + 1, :], (8, D))
    pl.semaphore_wait(barrier, NP - 1 + NZ - 1 + 1)

    def wpl_copy(k):
        return remote(w_ref, wpl.at[me], wpl_ss, wpl_rs, plane(mod(me + k, NP)))

    loop(1, NP, lambda k: wpl_copy(k).start())

    def qkv_copy(k, source, slot):
        peer = mod(f + k, FS)
        arrival = q_rs.at[k] if slot == 0 else kv_rs.at[slot - 1]
        return remote(source.at[:, at128(peer)], qkvh.at[slot, at128(f), :], qkv_ss, arrival, (peer, r))

    def go_down():
        return remote(go_ref.at[pl.ds(0, 16), :], gox.at[pl.ds(144, 16), :], go_ss.at[0], go_rs.at[0], (f - 1, r))

    def go_up():
        return remote(go_ref.at[pl.ds(112, 16), :], gox.at[pl.ds(0, 16), :], go_ss.at[1], go_rs.at[1], (f + 1, r))

    loop(1, FS, lambda k: qkv_copy(k, k_ref, 1).start())
    all_arrived(wpl.at[pl.ds(0, NP - 1)], wpl_rs)
    for p in range(NP):
        wtmp[4 * p : 4 * p + 4, :] = wpl[p].astype(F32)

    def wblock(c, zz):
        return pl.ds(pl.multiple_of(c * 512 + zz * 64, 64), 64)

    wbuf[wblock(core, z), :] = wtmp[...].astype(BF16)

    up, down = zline(mod(z + 1, NZ)), zline(mod(z + NZ - 1, NZ))

    def ag_part(part):
        return pl.ds(part * PART, PART)

    def ag_copy(way, s, part):
        block = mod(z - s + NZ, NZ) if way == 0 else mod(z + s, NZ)
        view = wbuf.at[wblock(core, block), ag_part(part)]
        return remote(view, view, ag_ss, ag_rs.at[way, s, part], up if way == 0 else down)

    def ag_arrived(way, s, part):
        block = mod(z - 1 - s + NZ, NZ) if way == 0 else mod(z + 1 + s, NZ)
        view = wbuf.at[wblock(core, block), ag_part(part)]
        remote(view, view, ag_ss, ag_rs.at[way, s, part], down if way == 0 else up).wait_recv()

    def agp_copy(k, part):
        view = wbuf.at[wblock(core, mod(z + k, NZ)), ag_part(part)]
        return remote(view, view, agp_ss, agp_rs.at[part], partner)

    def goes_far(way, s, part):
        return s < 3 or part % 2 == way

    def ag_first(*parts):
        for part in parts:
            for way in range(2):
                ag_copy(way, 0, part).start()
        for part in parts:
            agp_copy(0, part).start()

    def ag_turn(s, *parts):
        for part in parts:
            for way in range(2):
                if goes_far(way, s, part):
                    ag_arrived(way, s, part)
                    if s < 3 and goes_far(way, s + 1, part):
                        ag_copy(way, s + 1, part).start()
            if s < 3:
                agp_copy(NZ - 1 - s, part).start()
                agp_copy(1 + s, part).start()
            else:
                agp_copy(4, part).start()

    def agp_arrived(part):
        all_arrived(wbuf.at[pl.ds(0, 512), ag_part(part)], agp_rs.at[part])

    ag_first(0, 1, 2)
    loop(1, FS, lambda k: qkv_copy(k, v_ref, 2).start())
    loop(1, FS, lambda k: qkv_copy(FS - k, q_ref, 0).start())

    @pl.when(f > 0)
    def _():
        go_down().start()

    @pl.when(f < FS - 1)
    def _():
        go_up().start()

    ag_turn(0, 0, 1, 2)

    def query_arrived(source):
        arrival = q_rs.at[mod(f - source + FS, FS)]
        remote(q_ref.at[:, at128(source)], qkvh.at[0, at128(source), :], qkv_ss, arrival, (source, r)).wait_recv()

    for slot in (1, 2):
        all_arrived(qkvh.at[slot, pl.ds(0, 896), :], kv_rs.at[slot - 1])

    def ext(i):
        return pl.ds(pl.multiple_of(i * ROWS, ROWS), ROWS + 2 * HALO)

    def att_copy(k):
        peer = mod(f + k, FS)
        return remote(ohp.at[ext(peer), :], attx.at[:, at128(f)], att_ss, att_rs, (peer, r))

    first = lax.div(f, jnp.int32(2))

    def att_send(i):
        for half in range(2):
            peer = mod(2 * (first + i) - 1 + half + FS, FS)

            @pl.when(peer != f)
            def _():
                att_copy(mod(peer - f + FS, FS)).start()

    def attend(i):
        block = mod(first + i, SPAN // BLK)
        for half in range(2):
            source = 2 * block + half

            @pl.when(source != f)
            def _():
                query_arrived(source)

        rows = pl.ds(pl.multiple_of(block * BLK, BLK), BLK)
        scores = dot_nt(qkvh[0, rows, :], qkvh[1])
        exponent = jnp.exp2((scores - jnp.max(scores, axis=1, keepdims=True)) * EXP_SCALE)
        rounded = (exponent * (1.0 / jnp.sum(exponent, axis=1, keepdims=True))).astype(BF16)
        prob[rows, :] = rounded
        attended = jnp.dot(rounded, qkvh[2], preferred_element_type=F32)
        ohp[pl.ds(pl.multiple_of(block * BLK + HALO, HALO), BLK), :] = attended.astype(BF16)

        @pl.when(i > 0)
        def _():
            att_send(i)

        for part in range(3):

            @pl.when(i == part)
            def _():
                ag_turn(1, part)

    loop(0, SPAN // BLK, attend)
    att_send(SPAN // BLK)
    attx[:, at128(f)] = ohp[ext(f), :]
    ag_turn(2, 0, 1, 2)
    ag_first(3)
    ag_turn(3, 0)

    @pl.when(f < FS - 1)
    def _():
        remote(go_ref.at[pl.ds(0, 16), :], gox.at[pl.ds(144, 16), :], go_ss.at[0], go_rs.at[0], (f + 1, r)).wait_recv()

    @pl.when(f > 0)
    def _():
        remote(go_ref.at[pl.ds(112, 16), :], gox.at[pl.ds(0, 16), :], go_ss.at[1], go_rs.at[1], (f - 1, r)).wait_recv()

    all_arrived(attx.at[:, pl.ds(0, 896)], att_rs)
    attp[...] = jnp.dot(attx[...], perm[...], preferred_element_type=F32).astype(BF16)
    attt[...] = attp[HALO : HALO + ROWS, :].T
    ag_turn(3, 1)
    agp_arrived(0)
    grad_scale = 1.0 / math.sqrt(SPAN * 32)
    ga_acc[...] = jnp.zeros((ROWS, INNER), F32)
    tapg[KERNEL : KERNEL + 1, :] = jnp.zeros((1, D), F32)

    def rsp_copy(part):
        cols = pl.ds(pl.multiple_of(part * PART, PART), PART)
        rows = pl.ds(pl.multiple_of((1 - core) * 512, 512), 512)
        return remote(wgs.at[rows, cols], pbuf.at[:, cols], rsp_ss, rsp_rs.at[part], partner)

    def rsp_arrived(part):
        cols = pl.ds(part * PART, PART)
        rows = pl.ds(pl.multiple_of(core * 512, 512), 512)
        remote(wgs.at[rows, cols], pbuf.at[:, cols], rsp_ss, rsp_rs.at[part], partner).wait_recv()

    def ta_copy(k):
        peer = mod(me + k, NP)
        return remote(tapg.at[:, at128(peer)], ta.at[k], ta_ss, ta_rs, plane(peer))

    def takes_part(way, s, part):
        return s > 0 or (part % 2 == 1) == (way == 0)

    def rs_copy(way, s, part):
        view = (way, s, slice(None), pl.ds(part * PART, PART))
        return remote(
            sbuf.at[view], rbuf.at[view], rs_ss, rs_rs.at[way, s, part], up if way == 0 else down
        )

    def rs_arrived(way, s, part):
        view = (way, s, slice(None), pl.ds(part * PART, PART))
        remote(
            sbuf.at[view], rbuf.at[view], rs_ss, rs_rs.at[way, s, part], down if way == 0 else up
        ).wait_recv()

    def chip_sum(block, cols):
        return wgs[wblock(core, block), cols].astype(F32) + pbuf[at64(block), cols].astype(F32)

    def rs(s, part):
        cols = slice(part * PART, part * PART + PART)
        if s == 0:
            rsp_arrived(part)
        for way in range(2):
            if not takes_part(way, s, part):
                continue
            block = mod(z + 4 - s, NZ) if way == 0 else mod(z + 4 + s, NZ)
            value = chip_sum(block, cols)
            if s > 0 and takes_part(way, s - 1, part):
                rs_arrived(way, s - 1, part)
                value = value + rbuf[way, s - 1, :, cols].astype(F32)
            sbuf[way, s, :, cols] = value.astype(BF16)
            rs_copy(way, s, part).start()

    def pw_copy(part, k):
        peer = mod(me + k, NP)
        return remote(pw_s.at[part, peer], pw_r.at[part, k], pw_ss, pw_rs.at[part], plane(peer))

    def pz_copy(part, k):
        other = mod(z + k, NZ)
        return remote(pz_s.at[part, other], pz_r.at[part, k], pz_ss, pz_rs.at[part], zline(other))

    def early_give(part):
        rsp_arrived(part)

        def pack(zz):
            wtmp[:, 0:PART] = chip_sum(zz, slice(part * PART, part * PART + PART))
            for p in range(NP):
                pw_s[part, p, zz] = wtmp[4 * p : 4 * p + 4, 0:PART].astype(BF16)

        loop(0, NZ, pack)
        loop(1, NP, lambda k: pw_copy(part, k).start())

    def early_sum(part):
        all_arrived(pw_r.at[part, pl.ds(0, NP - 1)], pw_rs.at[part])

        def add(zz):
            total = pw_s[part, me, zz].astype(F32)
            for k in range(1, NP):
                total = total + pw_r[part, k, zz].astype(F32)
            pz_s[part, zz] = total.astype(BF16)

        loop(0, NZ, add)
        loop(1, NZ, lambda k: pz_copy(part, k).start())

    def early_end(part):
        all_arrived(pz_r.at[part, pl.ds(0, NZ - 1)], pz_rs.at[part])
        total = pz_s[part, z].astype(F32)
        for k in range(1, NZ):
            total = total + pz_r[part, k].astype(F32)
        o_wg[:, part * PART : part * PART + PART] = total * grad_scale

    def at_cols(c):
        return pl.ds(pl.multiple_of(c * COLS, COLS), COLS)

    def project(c):
        next_s[...] = jnp.dot(attp[...], wbuf[:, at_cols(c)], preferred_element_type=F32).astype(BF16).astype(F32)

    def pull_back(c):
        gp = last_s[...]
        wgs[:, at_cols(c)] = jnp.dot(attt[...], gp, preferred_element_type=F32).astype(BF16)
        ga_acc[...] += dot_nt(gp, wbuf[:, at_cols(c)])

    events = {
        0: ((ag_turn, 3, 2), (agp_arrived, 1)),
        1: ((ag_turn, 1, 3),),
        2: ((agp_arrived, 2),),
        3: ((ag_turn, 2, 3), (early_give, 0)),
        4: ((ag_turn, 3, 3), (agp_arrived, 3)),
        5: ((early_give, 1),),
        7: ((rs, 0, 2),),
    }

    def tap_grads(tile):
        here = at128(tile)
        gc_own = gc_all[:, here].reshape(16, 8, 128)
        for shift in range(8):
            moved = proj_all[shift : shift + 184, here]
            for j in range(KERNEL):
                if (17 + j) % 8 == shift:
                    start = 17 + j - shift
                    partial = jnp.sum(gc_own * moved[start : start + 128].reshape(16, 8, 128), axis=0)
                    tapg[j : j + 1, here] = jnp.sum(partial, axis=0, keepdims=True)

        @pl.when(tile != me)
        def _():
            ta_copy(mod(tile - me + NP, NP)).start()

    def columns(c):
        project(jnp.minimum(c + 1, D // COLS - 1))
        pull_back(jnp.maximum(c - 1, 0))
        for lane in range(COLS // 128):
            here = pl.ds(pl.multiple_of(c * COLS + lane * 128, 128), 128)
            local = slice(lane * 128, lane * 128 + 128)
            conv = jnp.zeros((20, 8, 128), F32)
            for shift in range(8):
                moved = proj_s[shift : shift + 184, local]
                for j in range(KERNEL):
                    if (1 + j) % 8 == shift:
                        start = 1 + j - shift
                        conv = conv + tapb[j, :, here][None] * moved[start : start + 160].reshape(20, 8, 128)
            conv = conv.reshape(160, 128)
            sig = jax.nn.sigmoid(conv)
            upstream = gox[:, here].astype(F32)
            o_block[:, here] = (proj_s[32:160, local] + conv[16:144] * sig[16:144]).astype(BF16)
            grad_conv = (upstream * sig * (1.0 + conv * (1.0 - sig))).astype(BF16).astype(F32)
            gc_s[:, local] = grad_conv
            gc_all[:, here] = grad_conv[16:144]
            total = gox[16:144, here].astype(F32).reshape(16, 8, 128)
            for shift in range(8):
                moved = gc_s[shift : shift + 152, local]
                for j in range(KERNEL):
                    if (31 - j) % 8 == shift:
                        start = 31 - j - shift
                        total = total + tapb[j, :, here][None] * moved[start : start + 128].reshape(16, 8, 128)
            gp_s[:, local] = total.reshape(128, 128).astype(BF16)
        proj_all[:, at_cols(c)] = proj_s[...]
        proj_s[...] = next_s[...]
        last_s[...] = gp_s[...]

        @pl.when((c > 0) & (mod(c, 2) == 0))
        def _():
            rsp_copy(lax.div(c, jnp.int32(2)) - 1).start()

        for at, calls in events.items():

            @pl.when(c == at)
            def _():
                for call, *given in calls:
                    call(*given)

    project(0)
    ag_turn(0, 3)
    proj_s[...] = next_s[...]
    last_s[...] = jnp.zeros((ROWS, COLS), BF16)
    loop(0, D // COLS, columns)
    pull_back(D // COLS - 1)
    rsp_copy(3).start()
    ga_s[...] = dot_nt(ga_acc[...].astype(BF16), perm[...]).astype(BF16)

    def ga_copy(k):
        peer = mod(f + k, FS)
        return remote(ga_s.at[:, at128(peer)], gh.at[at128(f), :], ga_ss, ga_rs, (peer, r))

    loop(1, FS, lambda k: ga_copy(k).start())

    gh[at128(f), :] = ga_s[:, at128(f)]
    loop(0, 4, tap_grads)
    rs(0, 3)
    rs(1, 2)
    loop(4, 10, tap_grads)
    early_sum(0)
    loop(10, NP, tap_grads)
    rs(1, 3)
    rs(2, 2)
    early_sum(1)
    dk_acc[...] = jnp.zeros((SPAN, HDIM), F32)
    dv_acc[...] = jnp.zeros((SPAN, HDIM), F32)

    def value_back(i):
        rows = pl.ds(pl.multiple_of(i * BLK, BLK), BLK)
        dv_acc[...] += dot_tn(prob[rows, :], gh[rows, :])

    outs = ((o_gq, 0), (o_gk, 1), (o_gv, 2))

    def d_copy(k, ref, slot):
        peer = mod(f + k, FS)
        return remote(dh.at[slot, at128(peer), :], ref.at[:, at128(f)], d_ss, d_rs.at[slot], (peer, r))

    def attend_back(i):
        i = mod(i + lax.div(f, jnp.int32(2)), SPAN // BLK)
        rows = pl.ds(pl.multiple_of(i * BLK, BLK), BLK)
        grad = gh[rows, :]
        rounded = prob[rows, :]
        weights = rounded.astype(F32)
        grad_probs = dot_nt(grad, qkvh[2])
        row_dot = jnp.sum(weights * grad_probs, axis=1, keepdims=True)
        grad_scores = (weights * (grad_probs - row_dot)).astype(BF16)
        dh[0, rows, :] = (jnp.dot(grad_scores, qkvh[1], preferred_element_type=F32) * INV_ROOT).astype(BF16)
        for half in range(2):
            peer = 2 * i + half

            @pl.when(peer != f)
            def _():
                d_copy(mod(peer - f + FS, FS), o_gq, 0).start()

        dk_acc[...] += dot_tn(grad_scores, qkvh[0, rows, :])

    def tp_copy():
        return remote(tp_s, tp_r, tp_ss, tp_rs, partner)

    def tb_copy(k):
        return remote(tb.at[z], tb.at[z], tb_ss, tb_rs, zline(mod(z + k, NZ)))

    def tc_copy(k):
        return remote(tc_s, tc.at[me], tc_ss, tc_rs, plane(mod(me + k, NP)))


    def wgp_copy(half, k):
        peer = mod(me + k, NP)
        return remote(wgp_s.at[half, peer], wgp_r.at[half, k], wgp_ss, wgp_rs.at[half], plane(peer))

    def settle(half):
        for part in (2 * half, 2 * half + 1):
            cols = slice(part * PART, part * PART + PART)
            rs_arrived(0, 3, part)
            rs_arrived(1, 3, part)
            wtmp[:, cols] = chip_sum(z, cols) + rbuf[0, 3, :, cols].astype(F32) + rbuf[1, 3, :, cols].astype(F32)
        for p in range(NP):
            wgp_s[half, p] = wtmp[4 * p : 4 * p + 4, half * 1024 : half * 1024 + 1024].astype(BF16)
        loop(1, NP, lambda k: wgp_copy(half, k).start())

    all_arrived(gh.at[pl.ds(0, 896), :], ga_rs)
    loop(0, SPAN // BLK, value_back)
    dh[2] = dv_acc[...].astype(BF16)
    loop(1, FS, lambda k: d_copy(k, o_gv, 2).start())
    loop(0, 1, attend_back)
    rs(2, 3)
    rs(3, 2)
    all_arrived(ta.at[pl.ds(0, NP - 1)], ta_rs)
    total = tapg[:, at128(me)]
    for k in range(1, NP):
        total = total + ta[k]
    tp_s[...] = total
    tp_copy().start()
    loop(1, 2, attend_back)
    tp_copy().wait_recv()
    tb[z] = (tp_s[...] + tp_r[...]).astype(BF16)
    loop(1, NZ, lambda k: tb_copy(k).start())
    loop(2, 4, attend_back)
    dh[1] = (dk_acc[...] * INV_ROOT).astype(BF16)

    loop(1, FS, lambda k: d_copy(k, o_gk, 1).start())
    for ref, slot in outs:
        ref[:, at128(f)] = dh[slot, at128(f), :]
    rs(3, 3)
    early_end(0)
    early_end(1)
    all_arrived(tb.at[pl.ds(0, NZ - 1)], tb_rs)
    total = tb[0].astype(F32)
    for k in range(1, NZ):
        total = total + tb[k].astype(F32)
    tc_s[...] = (total * grad_scale).astype(BF16)
    loop(1, NP, lambda k: tc_copy(k).start())
    tc[me] = tc_s[...]
    settle(1)
    for ref, slot in outs:
        all_arrived(ref.at[:, pl.ds(0, 896)], d_rs.at[slot])
    all_arrived(wgp_r.at[1, pl.ds(0, NP - 1)], wgp_rs.at[1])
    total = wgp_s[1, me].astype(F32)
    for k in range(1, NP):
        total = total + wgp_r[1, k].astype(F32)
    o_wg[:, 1024:D] = total * grad_scale
    all_arrived(tc.at[pl.ds(0, NP - 1)], tc_rs)
    for p in range(NP):
        o_cg[:, p * 128 : p * 128 + 128] = tc[p].astype(F32)[0:KERNEL]

    all_sent(wpl.at[pl.ds(0, NP - 1)], wpl_ss)
    all_sent(qkvh.at[:, pl.ds(0, 896), :], qkv_ss)
    all_sent(wbuf.at[pl.ds(0, 448), :], ag_ss)
    all_sent(wbuf.at[pl.ds(0, 512), :], agp_ss)
    all_sent(attx.at[:, pl.ds(0, 896)], att_ss)
    all_sent(ga_s.at[:, pl.ds(0, 896)], ga_ss)
    all_sent(pbuf, rsp_ss)
    all_sent(wbuf.at[pl.ds(0, 224), :], rs_ss)
    all_sent(pw_s.at[:, pl.ds(0, NP - 1)], pw_ss)
    all_sent(pz_s.at[:, pl.ds(0, NZ - 1)], pz_ss)
    all_sent(dh.at[:, pl.ds(0, 896), :], d_ss)
    all_sent(wgp_s.at[1, pl.ds(0, NP - 1)], wgp_ss)
    all_sent(ta.at[pl.ds(0, NP - 1)], ta_ss)
    all_sent(tb.at[pl.ds(0, NZ - 1)], tb_ss)
    all_sent(tc.at[pl.ds(0, NP - 1)], tc_ss)
    tp_copy().wait_send()

    @pl.when(f > 0)
    def _():
        go_down().wait_send()

    @pl.when(f < FS - 1)
    def _():
        go_up().wait_send()


def put_out(*refs):
    sources, targets, sems = refs[:6], refs[6:12], refs[12]
    copies = [pltpu.make_async_copy(sources[i], targets[i], sems.at[i]) for i in range(6)]
    for copy in copies:
        copy.start()
    for copy in copies:
        copy.wait()


def shards(queries, key_rows, value_rows, out_weight, conv_weight, grad_out):
    vmem = pl.BlockSpec(memory_space=pltpu.VMEM)
    hbm = pl.BlockSpec(memory_space=pltpu.HBM)
    anywhere = pl.BlockSpec(memory_space=pl.ANY)
    dma = pltpu.SemaphoreType.DMA
    results = (
        ((ROWS, D), BF16),
        ((ROWS, INNER), BF16),
        ((ROWS, INNER), BF16),
        ((ROWS, INNER), BF16),
        ((4, D), F32),
        ((KERNEL, D), F32),
    )
    shapes = tuple(jax.ShapeDtypeStruct(*result) for result in results)
    found = pl.pallas_call(
        kernel,
        out_shape=shapes,
        in_specs=[hbm] * 6,
        out_specs=(vmem,) * 6,
        scratch_shapes=[
            pltpu.VMEM((3, SPAN, HDIM), BF16),
            pltpu.VMEM((SPAN, SPAN), BF16),
            pltpu.VMEM((SPAN + 2 * HALO, HDIM), BF16),
            pltpu.VMEM((ROWS + 2 * HALO, INNER), BF16),
            pltpu.VMEM((NP, 4, D), BF16),
            pltpu.VMEM((64, D), F32),
            pltpu.VMEM((INNER, D), BF16),
            pltpu.VMEM((INNER, INNER), BF16),
            pltpu.VMEM((ROWS + 2 * HALO, INNER), BF16),
            pltpu.VMEM((INNER, ROWS), BF16),
            pltpu.VMEM((160, D), BF16),
            pltpu.VMEM((KERNEL, D), BF16),
            pltpu.VMEM((KERNEL, 8, D), F32),
            pltpu.VMEM((ROWS + 2 * HALO, COLS), F32),
            pltpu.VMEM((ROWS + 2 * HALO, COLS), F32),
            pltpu.VMEM((ROWS + 2 * HALO, D), F32),
            pltpu.VMEM((160, COLS), F32),
            pltpu.VMEM((ROWS, D), F32),
            pltpu.VMEM((ROWS, COLS), BF16),
            pltpu.VMEM((ROWS, COLS), BF16),
            pltpu.VMEM((INNER, D), BF16),
            pltpu.VMEM((ROWS, INNER), F32),
            pltpu.VMEM((ROWS, INNER), BF16),
            pltpu.VMEM((SPAN, HDIM), BF16),
            pltpu.VMEM((3, SPAN, HDIM), BF16),
            pltpu.VMEM((SPAN, HDIM), F32),
            pltpu.VMEM((SPAN, HDIM), F32),
            pltpu.VMEM((512, D), BF16),
            pltpu.VMEM((2, 4, 64, D), BF16),
            pltpu.VMEM((2, 4, 64, D), BF16),
            pltpu.VMEM((2, NP, 4, 1024), BF16),
            pltpu.VMEM((2, NP, 4, 1024), BF16),
            pltpu.VMEM((2, NP, NZ, 4, PART), BF16),
            pltpu.VMEM((2, NP, NZ, 4, PART), BF16),
            pltpu.VMEM((2, NZ, 4, PART), BF16),
            pltpu.VMEM((2, NZ, 4, PART), BF16),
            pltpu.VMEM((32, D), F32),
            pltpu.VMEM((NP, 32, 128), F32),
            pltpu.VMEM((32, 128), F32),
            pltpu.VMEM((32, 128), F32),
            pltpu.VMEM((NZ, 32, 128), BF16),
            pltpu.VMEM((32, 128), BF16),
            pltpu.VMEM((NP, 32, 128), BF16),
            dma((6,)),
            dma, dma((FS,)), dma((2,)),
            dma, dma,
            dma((2,)), dma((2,)),
            dma, dma((2, 4, 4)),
            dma, dma((4,)),
            dma, dma,
            dma, dma,
            dma, dma((4,)),
            dma, dma((2, 4, 4)),
            dma, dma((3,)),
            dma, dma((2,)),
            dma, dma((2,)),
            dma, dma((2,)),
            dma, dma,
            dma, dma,
            dma, dma,
            dma, dma,
        ],
        compiler_params=pltpu.CompilerParams(
            collective_id=0, has_side_effects=True, vmem_limit_bytes=50 * 1024 * 1024
        ),
    )(
        *(
            pltpu.with_memory_space_constraint(given, pltpu.HBM)
            for given in (queries[0], key_rows[0], value_rows[0], out_weight, conv_weight, grad_out[0])
        )
    )
    block_out, grad_queries, grad_keys, grad_values, weight_grad, conv_grad = pl.pallas_call(
        put_out,
        out_shape=shapes,
        in_specs=[anywhere] * 6,
        out_specs=(hbm,) * 6,
        scratch_shapes=[dma((6,))],
        compiler_params=pltpu.CompilerParams(vmem_limit_bytes=8 * 1024 * 1024),
    )(*found)
    return (block_out[None], grad_queries[None], grad_keys[None], grad_values[None], weight_grad, conv_grad)


def solution(mesh):
    return jax.shard_map(
        shards,
        mesh=mesh,
        in_specs=(
            P("frame", "fsdp", None),
            P("frame", "fsdp", None),
            P("frame", "fsdp", None),
            P(("fsdp", "frame"), None),
            P(),
            P("frame", "fsdp", None),
        ),
        out_specs=(
            P("frame", "fsdp", None),
            P("frame", "fsdp", None),
            P("frame", "fsdp", None),
            P("frame", "fsdp", None),
            P(("fsdp", "frame"), None),
            P(),
        ),
        check_vma=False,
    )
```

```python
import math

import jax
import jax.numpy as jnp
from jax import lax
from jax.experimental import pallas as pl
from jax.experimental.pallas import tpu as pltpu
from jax.sharding import PartitionSpec as P

MESH = pl.DeviceIdType.MESH
HDIM = 128
KERNEL = 31
ROWS = 128
INNER = 1024
D = 2048
SPAN = 1024
FS = 8
NZ = 8
NP = 16
HALO = 32
COLS = 256
PART = 512
BLK = 256
INV_ROOT = 1.0 / math.sqrt(HDIM)
EXP_SCALE = INV_ROOT * math.log2(math.e)
F32 = jnp.float32
BF16 = jnp.bfloat16


def mod(a, n):
    return lax.rem(a, jnp.int32(n))


def remote(src, dst, send, recv, device):
    return pltpu.make_async_remote_copy(
        src_ref=src, dst_ref=dst, send_sem=send, recv_sem=recv, device_id=device, device_id_type=MESH
    )


def loop(lower, upper, body):
    def step(i, carry):
        body(i)
        return carry

    lax.fori_loop(lower, upper, step, 0)


def at128(i):
    return pl.ds(pl.multiple_of(i * 128, 128), 128)


def at64(i):
    return pl.ds(pl.multiple_of(i * 64, 64), 64)


def dot_nt(a, b):
    return lax.dot_general(a, b, (((1,), (1,)), ((), ())), preferred_element_type=F32)


def dot_tn(a, b):
    return lax.dot_general(a, b, (((0,), (0,)), ((), ())), preferred_element_type=F32)


def kernel(
    q_ref, k_ref, v_ref, w_ref, taps_ref, go_ref,
    o_block, o_gq, o_gk, o_gv, o_wg, o_cg,
    qkvh, prob, ohp, attx, wpl, wtmp, wbuf, perm, attp, attt, gox, tapv, tapb, proj_s, next_s, proj_all, gc_s, gc_all, gp_s, last_s, wgs,
    ga_acc, ga_s, gh, dh, dk_acc, dv_acc, pbuf, sbuf, rbuf, wgp_s, wgp_r, pw_s, pw_r, pz_s, pz_r,
    tapg, ta, tp_s, tp_r, tb, tc_s, tc,
    own_s, qkv_ss, q_rs, kv_rs, wpl_ss, wpl_rs, go_ss, go_rs, ag_ss, ag_rs, agp_ss, agp_rs, att_ss, att_rs,
    ga_ss, ga_rs, rsp_ss, rsp_rs, rs_ss, rs_rs, d_ss, d_rs, wgp_ss, wgp_rs, pw_ss, pw_rs, pz_ss, pz_rs,
    ta_ss, ta_rs, tp_ss, tp_rs, tb_ss, tb_rs, tc_ss, tc_rs,
):
    f = lax.axis_index("fsdp").astype(jnp.int32)
    r = lax.axis_index("frame").astype(jnp.int32)
    ylo = lax.div(r, jnp.int32(16))
    z = mod(lax.div(r, jnp.int32(2)), NZ)
    core = mod(r, 2)
    me = f * 2 + ylo

    def plane(p):
        return (lax.div(p, jnp.int32(2)), mod(p, 2) * 16 + z * 2 + core)

    def zline(other):
        return (f, ylo * 16 + other * 2 + core)

    partner = (f, ylo * 16 + z * 2 + 1 - core)

    def all_arrived(ref, sem):
        remote(ref, ref, sem, sem, partner).wait_recv()

    def all_sent(ref, sem):
        remote(ref, ref, sem, sem, partner).wait_send()

    heads = ((q_ref, 0), (k_ref, 1), (v_ref, 2))

    def own_copies():
        for source, slot in heads:
            yield pltpu.make_async_copy(source.at[:, at128(f)], qkvh.at[slot, at128(f), :], own_s.at[slot])
        yield pltpu.make_async_copy(go_ref, gox.at[pl.ds(16, ROWS), :], own_s.at[3])
        yield pltpu.make_async_copy(w_ref, wpl.at[me], own_s.at[4])
        yield pltpu.make_async_copy(taps_ref, tapv, own_s.at[5])

    barrier = pltpu.get_barrier_semaphore()

    def greet_plane(k):
        pl.semaphore_signal(barrier, inc=1, device_id=plane(mod(me + k, NP)), device_id_type=MESH)

    def greet_z(k):
        pl.semaphore_signal(barrier, inc=1, device_id=zline(mod(z + k, NZ)), device_id_type=MESH)

    loop(1, NP, greet_plane)
    loop(1, NZ, greet_z)
    pl.semaphore_signal(barrier, inc=1, device_id=partner, device_id_type=MESH)
    for copy in own_copies():
        copy.start()

    @pl.when(f == 0)
    def _():
        gox[0:16, :] = jnp.zeros((16, D), BF16)

    @pl.when(f == FS - 1)
    def _():
        gox[144:160, :] = jnp.zeros((16, D), BF16)

    ohp[0:HALO, :] = jnp.zeros((HALO, HDIM), BF16)
    ohp[HALO + SPAN : HALO + SPAN + HALO, :] = jnp.zeros((HALO, HDIM), BF16)

    def perm_rows(b):
        row = lax.broadcasted_iota(jnp.int32, (128, INNER), 0) + b * 128
        col = lax.broadcasted_iota(jnp.int32, (128, INNER), 1)
        at = ((col >> 2) & 15) * 64 + ((col >> 6) & 7) * 8 + (col >> 9) * 4 + (col & 3)
        perm[at128(b), :] = jnp.where(row == at, 1.0, 0.0).astype(BF16)

    loop(0, 8, perm_rows)
    for copy in own_copies():
        copy.wait()
    taps = tapv[...].astype(F32)
    for j in range(KERNEL):
        tapb[j] = jnp.broadcast_to(taps[j : j + 1, :], (8, D))
    pl.semaphore_wait(barrier, NP - 1 + NZ - 1 + 1)

    def wpl_copy(k):
        return remote(w_ref, wpl.at[me], wpl_ss, wpl_rs, plane(mod(me + k, NP)))

    loop(1, NP, lambda k: wpl_copy(k).start())

    def qkv_copy(k, source, slot):
        peer = mod(f + k, FS)
        arrival = q_rs.at[k] if slot == 0 else kv_rs.at[slot - 1]
        return remote(source.at[:, at128(peer)], qkvh.at[slot, at128(f), :], qkv_ss, arrival, (peer, r))

    def go_down():
        return remote(go_ref.at[pl.ds(0, 16), :], gox.at[pl.ds(144, 16), :], go_ss.at[0], go_rs.at[0], (f - 1, r))

    def go_up():
        return remote(go_ref.at[pl.ds(112, 16), :], gox.at[pl.ds(0, 16), :], go_ss.at[1], go_rs.at[1], (f + 1, r))

    loop(1, FS, lambda k: qkv_copy(k, k_ref, 1).start())
    all_arrived(wpl.at[pl.ds(0, NP - 1)], wpl_rs)
    for p in range(NP):
        wtmp[4 * p : 4 * p + 4, :] = wpl[p].astype(F32)

    def wblock(c, zz):
        return pl.ds(pl.multiple_of(c * 512 + zz * 64, 64), 64)

    wbuf[wblock(core, z), :] = wtmp[...].astype(BF16)

    up, down = zline(mod(z + 1, NZ)), zline(mod(z + NZ - 1, NZ))

    def ag_part(part):
        return pl.ds(part * PART, PART)

    def ag_copy(way, s, part):
        block = mod(z - s + NZ, NZ) if way == 0 else mod(z + s, NZ)
        view = wbuf.at[wblock(core, block), ag_part(part)]
        return remote(view, view, ag_ss, ag_rs.at[way, s, part], up if way == 0 else down)

    def ag_arrived(way, s, part):
        block = mod(z - 1 - s + NZ, NZ) if way == 0 else mod(z + 1 + s, NZ)
        view = wbuf.at[wblock(core, block), ag_part(part)]
        remote(view, view, ag_ss, ag_rs.at[way, s, part], down if way == 0 else up).wait_recv()

    def agp_copy(k, part):
        view = wbuf.at[wblock(core, mod(z + k, NZ)), ag_part(part)]
        return remote(view, view, agp_ss, agp_rs.at[part], partner)

    def goes_far(way, s, part):
        return s < 3 or part % 2 == way

    def ag_first(*parts):
        for part in parts:
            for way in range(2):
                ag_copy(way, 0, part).start()
        for part in parts:
            agp_copy(0, part).start()

    def ag_turn(s, *parts):
        for part in parts:
            for way in range(2):
                if goes_far(way, s, part):
                    ag_arrived(way, s, part)
                    if s < 3 and goes_far(way, s + 1, part):
                        ag_copy(way, s + 1, part).start()
            if s < 3:
                agp_copy(NZ - 1 - s, part).start()
                agp_copy(1 + s, part).start()
            else:
                agp_copy(4, part).start()

    def agp_arrived(part):
        all_arrived(wbuf.at[pl.ds(0, 512), ag_part(part)], agp_rs.at[part])

    ag_first(0, 1, 2)
    loop(1, FS, lambda k: qkv_copy(k, v_ref, 2).start())
    loop(1, FS, lambda k: qkv_copy(FS - k, q_ref, 0).start())

    @pl.when(f > 0)
    def _():
        go_down().start()

    @pl.when(f < FS - 1)
    def _():
        go_up().start()

    ag_turn(0, 0, 1, 2)

    def query_arrived(source):
        arrival = q_rs.at[mod(f - source + FS, FS)]
        remote(q_ref.at[:, at128(source)], qkvh.at[0, at128(source), :], qkv_ss, arrival, (source, r)).wait_recv()

    for slot in (1, 2):
        all_arrived(qkvh.at[slot, pl.ds(0, 896), :], kv_rs.at[slot - 1])

    def ext(i):
        return pl.ds(pl.multiple_of(i * ROWS, ROWS), ROWS + 2 * HALO)

    def att_copy(k):
        peer = mod(f + k, FS)
        return remote(ohp.at[ext(peer), :], attx.at[:, at128(f)], att_ss, att_rs, (peer, r))

    first = lax.div(f, jnp.int32(2))

    def att_send(i):
        for half in range(2):
            peer = mod(2 * (first + i) - 1 + half + FS, FS)

            @pl.when(peer != f)
            def _():
                att_copy(mod(peer - f + FS, FS)).start()

    def attend(i):
        block = mod(first + i, SPAN // BLK)
        for half in range(2):
            source = 2 * block + half

            @pl.when(source != f)
            def _():
                query_arrived(source)

        rows = pl.ds(pl.multiple_of(block * BLK, BLK), BLK)
        scores = dot_nt(qkvh[0, rows, :], qkvh[1])
        exponent = jnp.exp2((scores - jnp.max(scores, axis=1, keepdims=True)) * EXP_SCALE)
        rounded = (exponent * (1.0 / jnp.sum(exponent, axis=1, keepdims=True))).astype(BF16)
        prob[rows, :] = rounded
        attended = jnp.dot(rounded, qkvh[2], preferred_element_type=F32)
        ohp[pl.ds(pl.multiple_of(block * BLK + HALO, HALO), BLK), :] = attended.astype(BF16)

        @pl.when(i > 0)
        def _():
            att_send(i)

        for part in range(3):

            @pl.when(i == part)
            def _():
                ag_turn(1, part)

    loop(0, SPAN // BLK, attend)
    att_send(SPAN // BLK)
    attx[:, at128(f)] = ohp[ext(f), :]
    ag_turn(2, 0, 1, 2)
    ag_first(3)
    ag_turn(3, 0)

    @pl.when(f < FS - 1)
    def _():
        remote(go_ref.at[pl.ds(0, 16), :], gox.at[pl.ds(144, 16), :], go_ss.at[0], go_rs.at[0], (f + 1, r)).wait_recv()

    @pl.when(f > 0)
    def _():
        remote(go_ref.at[pl.ds(112, 16), :], gox.at[pl.ds(0, 16), :], go_ss.at[1], go_rs.at[1], (f - 1, r)).wait_recv()

    all_arrived(attx.at[:, pl.ds(0, 896)], att_rs)
    attp[...] = jnp.dot(attx[...], perm[...], preferred_element_type=F32).astype(BF16)
    attt[...] = attp[HALO : HALO + ROWS, :].T
    ag_turn(3, 1)
    agp_arrived(0)
    grad_scale = 1.0 / math.sqrt(SPAN * 32)
    ga_acc[...] = jnp.zeros((ROWS, INNER), F32)
    tapg[KERNEL : KERNEL + 1, :] = jnp.zeros((1, D), F32)

    def rsp_copy(part):
        cols = pl.ds(pl.multiple_of(part * PART, PART), PART)
        rows = pl.ds(pl.multiple_of((1 - core) * 512, 512), 512)
        return remote(wgs.at[rows, cols], pbuf.at[:, cols], rsp_ss, rsp_rs.at[part], partner)

    def rsp_arrived(part):
        cols = pl.ds(part * PART, PART)
        rows = pl.ds(pl.multiple_of(core * 512, 512), 512)
        remote(wgs.at[rows, cols], pbuf.at[:, cols], rsp_ss, rsp_rs.at[part], partner).wait_recv()

    def ta_copy(k):
        peer = mod(me + k, NP)
        return remote(tapg.at[:, at128(peer)], ta.at[k], ta_ss, ta_rs, plane(peer))

    def takes_part(way, s, part):
        return s > 0 or (part % 2 == 1) == (way == 0)

    def rs_copy(way, s, part):
        view = (way, s, slice(None), pl.ds(part * PART, PART))
        return remote(
            sbuf.at[view], rbuf.at[view], rs_ss, rs_rs.at[way, s, part], up if way == 0 else down
        )

    def rs_arrived(way, s, part):
        view = (way, s, slice(None), pl.ds(part * PART, PART))
        remote(
            sbuf.at[view], rbuf.at[view], rs_ss, rs_rs.at[way, s, part], down if way == 0 else up
        ).wait_recv()

    def chip_sum(block, cols):
        return wgs[wblock(core, block), cols].astype(F32) + pbuf[at64(block), cols].astype(F32)

    def rs(s, part):
        cols = slice(part * PART, part * PART + PART)
        if s == 0:
            rsp_arrived(part)
        for way in range(2):
            if not takes_part(way, s, part):
                continue
            block = mod(z + 4 - s, NZ) if way == 0 else mod(z + 4 + s, NZ)
            value = chip_sum(block, cols)
            if s > 0 and takes_part(way, s - 1, part):
                rs_arrived(way, s - 1, part)
                value = value + rbuf[way, s - 1, :, cols].astype(F32)
            sbuf[way, s, :, cols] = value.astype(BF16)
            rs_copy(way, s, part).start()

    def pw_copy(part, k):
        peer = mod(me + k, NP)
        return remote(pw_s.at[part, peer], pw_r.at[part, k], pw_ss, pw_rs.at[part], plane(peer))

    def pz_copy(part, k):
        other = mod(z + k, NZ)
        return remote(pz_s.at[part, other], pz_r.at[part, k], pz_ss, pz_rs.at[part], zline(other))

    def early_give(part):
        rsp_arrived(part)

        def pack(zz):
            wtmp[:, 0:PART] = chip_sum(zz, slice(part * PART, part * PART + PART))
            for p in range(NP):
                pw_s[part, p, zz] = wtmp[4 * p : 4 * p + 4, 0:PART].astype(BF16)

        loop(0, NZ, pack)
        loop(1, NP, lambda k: pw_copy(part, k).start())

    def early_sum(part):
        all_arrived(pw_r.at[part, pl.ds(0, NP - 1)], pw_rs.at[part])

        def add(zz):
            total = pw_s[part, me, zz].astype(F32)
            for k in range(1, NP):
                total = total + pw_r[part, k, zz].astype(F32)
            pz_s[part, zz] = total.astype(BF16)

        loop(0, NZ, add)
        loop(1, NZ, lambda k: pz_copy(part, k).start())

    def early_end(part):
        all_arrived(pz_r.at[part, pl.ds(0, NZ - 1)], pz_rs.at[part])
        total = pz_s[part, z].astype(F32)
        for k in range(1, NZ):
            total = total + pz_r[part, k].astype(F32)
        o_wg[:, part * PART : part * PART + PART] = total * grad_scale

    def at_cols(c):
        return pl.ds(pl.multiple_of(c * COLS, COLS), COLS)

    def project(c):
        next_s[...] = jnp.dot(attp[...], wbuf[:, at_cols(c)], preferred_element_type=F32).astype(BF16).astype(F32)

    def pull_back(c):
        gp = last_s[...]
        wgs[:, at_cols(c)] = jnp.dot(attt[...], gp, preferred_element_type=F32).astype(BF16)
        ga_acc[...] += dot_nt(gp, wbuf[:, at_cols(c)])

    events = {
        0: ((ag_turn, 3, 2), (agp_arrived, 1)),
        1: ((ag_turn, 1, 3),),
        2: ((agp_arrived, 2),),
        3: ((ag_turn, 2, 3), (early_give, 0)),
        4: ((ag_turn, 3, 3), (agp_arrived, 3), (early_give, 1)),
        7: ((rs, 0, 2),),
    }

    def tap_grads(tile):
        here = at128(tile)
        gc_own = gc_all[:, here].reshape(16, 8, 128)
        for shift in range(8):
            moved = proj_all[shift : shift + 184, here]
            for j in range(KERNEL):
                if (17 + j) % 8 == shift:
                    start = 17 + j - shift
                    partial = jnp.sum(gc_own * moved[start : start + 128].reshape(16, 8, 128), axis=0)
                    tapg[j : j + 1, here] = jnp.sum(partial, axis=0, keepdims=True)

        @pl.when(tile != me)
        def _():
            ta_copy(mod(tile - me + NP, NP)).start()

    def columns(c):
        project(jnp.minimum(c + 1, D // COLS - 1))
        pull_back(jnp.maximum(c - 1, 0))
        for lane in range(COLS // 128):
            here = pl.ds(pl.multiple_of(c * COLS + lane * 128, 128), 128)
            local = slice(lane * 128, lane * 128 + 128)
            conv = jnp.zeros((20, 8, 128), F32)
            for shift in range(8):
                moved = proj_s[shift : shift + 184, local]
                for j in range(KERNEL):
                    if (1 + j) % 8 == shift:
                        start = 1 + j - shift
                        conv = conv + tapb[j, :, here][None] * moved[start : start + 160].reshape(20, 8, 128)
            conv = conv.reshape(160, 128)
            sig = jax.nn.sigmoid(conv)
            upstream = gox[:, here].astype(F32)
            o_block[:, here] = (proj_s[32:160, local] + conv[16:144] * sig[16:144]).astype(BF16)
            grad_conv = (upstream * sig * (1.0 + conv * (1.0 - sig))).astype(BF16).astype(F32)
            gc_s[:, local] = grad_conv
            gc_all[:, here] = grad_conv[16:144]
            total = gox[16:144, here].astype(F32).reshape(16, 8, 128)
            for shift in range(8):
                moved = gc_s[shift : shift + 152, local]
                for j in range(KERNEL):
                    if (31 - j) % 8 == shift:
                        start = 31 - j - shift
                        total = total + tapb[j, :, here][None] * moved[start : start + 128].reshape(16, 8, 128)
            gp_s[:, local] = total.reshape(128, 128).astype(BF16)
        proj_all[:, at_cols(c)] = proj_s[...]
        proj_s[...] = next_s[...]
        last_s[...] = gp_s[...]

        @pl.when((c > 0) & (mod(c, 2) == 0))
        def _():
            rsp_copy(lax.div(c, jnp.int32(2)) - 1).start()

        for at, calls in events.items():

            @pl.when(c == at)
            def _():
                for call, *given in calls:
                    call(*given)

    project(0)
    ag_turn(0, 3)
    proj_s[...] = next_s[...]
    last_s[...] = jnp.zeros((ROWS, COLS), BF16)
    loop(0, D // COLS, columns)
    pull_back(D // COLS - 1)
    rsp_copy(3).start()
    ga_s[...] = dot_nt(ga_acc[...].astype(BF16), perm[...]).astype(BF16)

    def ga_copy(k):
        peer = mod(f + k, FS)
        return remote(ga_s.at[:, at128(peer)], gh.at[at128(f), :], ga_ss, ga_rs, (peer, r))

    loop(1, FS, lambda k: ga_copy(k).start())

    gh[at128(f), :] = ga_s[:, at128(f)]
    loop(0, 4, tap_grads)
    rs(0, 3)
    rs(1, 2)
    loop(4, 10, tap_grads)
    early_sum(0)
    loop(10, NP, tap_grads)
    rs(1, 3)
    rs(2, 2)
    early_sum(1)
    dk_acc[...] = jnp.zeros((SPAN, HDIM), F32)
    dv_acc[...] = jnp.zeros((SPAN, HDIM), F32)

    def value_back(i):
        rows = pl.ds(pl.multiple_of(i * BLK, BLK), BLK)
        dv_acc[...] += dot_tn(prob[rows, :], gh[rows, :])

    outs = ((o_gq, 0), (o_gk, 1), (o_gv, 2))

    def d_copy(k, ref, slot):
        peer = mod(f + k, FS)
        return remote(dh.at[slot, at128(peer), :], ref.at[:, at128(f)], d_ss, d_rs.at[slot], (peer, r))

    def attend_back(i):
        i = mod(i + lax.div(f, jnp.int32(2)), SPAN // BLK)
        rows = pl.ds(pl.multiple_of(i * BLK, BLK), BLK)
        grad = gh[rows, :]
        rounded = prob[rows, :]
        weights = rounded.astype(F32)
        grad_probs = dot_nt(grad, qkvh[2])
        row_dot = jnp.sum(weights * grad_probs, axis=1, keepdims=True)
        grad_scores = (weights * (grad_probs - row_dot)).astype(BF16)
        dh[0, rows, :] = (jnp.dot(grad_scores, qkvh[1], preferred_element_type=F32) * INV_ROOT).astype(BF16)
        for half in range(2):
            peer = 2 * i + half

            @pl.when(peer != f)
            def _():
                d_copy(mod(peer - f + FS, FS), o_gq, 0).start()

        dk_acc[...] += dot_tn(grad_scores, qkvh[0, rows, :])

    def tp_copy():
        return remote(tp_s, tp_r, tp_ss, tp_rs, partner)

    def tb_copy(k):
        return remote(tb.at[z], tb.at[z], tb_ss, tb_rs, zline(mod(z + k, NZ)))

    def tc_copy(k):
        return remote(tc_s, tc.at[me], tc_ss, tc_rs, plane(mod(me + k, NP)))


    def wgp_copy(half, k):
        peer = mod(me + k, NP)
        return remote(wgp_s.at[half, peer], wgp_r.at[half, k], wgp_ss, wgp_rs.at[half], plane(peer))

    def settle(half):
        for part in (2 * half, 2 * half + 1):
            cols = slice(part * PART, part * PART + PART)
            rs_arrived(0, 3, part)
            rs_arrived(1, 3, part)
            wtmp[:, cols] = chip_sum(z, cols) + rbuf[0, 3, :, cols].astype(F32) + rbuf[1, 3, :, cols].astype(F32)
        for p in range(NP):
            wgp_s[half, p] = wtmp[4 * p : 4 * p + 4, half * 1024 : half * 1024 + 1024].astype(BF16)
        loop(1, NP, lambda k: wgp_copy(half, k).start())

    all_arrived(gh.at[pl.ds(0, 896), :], ga_rs)
    loop(0, SPAN // BLK, value_back)
    dh[2] = dv_acc[...].astype(BF16)
    loop(1, FS, lambda k: d_copy(k, o_gv, 2).start())
    loop(0, 1, attend_back)
    rs(2, 3)
    rs(3, 2)
    all_arrived(ta.at[pl.ds(0, NP - 1)], ta_rs)
    total = tapg[:, at128(me)]
    for k in range(1, NP):
        total = total + ta[k]
    tp_s[...] = total
    tp_copy().start()
    loop(1, 2, attend_back)
    tp_copy().wait_recv()
    tb[z] = (tp_s[...] + tp_r[...]).astype(BF16)
    loop(1, NZ, lambda k: tb_copy(k).start())
    loop(2, 4, attend_back)
    dh[1] = (dk_acc[...] * INV_ROOT).astype(BF16)

    loop(1, FS, lambda k: d_copy(k, o_gk, 1).start())
    for ref, slot in outs:
        ref[:, at128(f)] = dh[slot, at128(f), :]
    rs(3, 3)
    early_end(0)
    early_end(1)
    all_arrived(tb.at[pl.ds(0, NZ - 1)], tb_rs)
    total = tb[0].astype(F32)
    for k in range(1, NZ):
        total = total + tb[k].astype(F32)
    tc_s[...] = (total * grad_scale).astype(BF16)
    loop(1, NP, lambda k: tc_copy(k).start())
    tc[me] = tc_s[...]
    settle(1)
    for ref, slot in outs:
        all_arrived(ref.at[:, pl.ds(0, 896)], d_rs.at[slot])
    all_arrived(wgp_r.at[1, pl.ds(0, NP - 1)], wgp_rs.at[1])
    total = wgp_s[1, me].astype(F32)
    for k in range(1, NP):
        total = total + wgp_r[1, k].astype(F32)
    o_wg[:, 1024:D] = total * grad_scale
    all_arrived(tc.at[pl.ds(0, NP - 1)], tc_rs)
    for p in range(NP):
        o_cg[:, p * 128 : p * 128 + 128] = tc[p].astype(F32)[0:KERNEL]

    all_sent(wpl.at[pl.ds(0, NP - 1)], wpl_ss)
    all_sent(qkvh.at[:, pl.ds(0, 896), :], qkv_ss)
    all_sent(wbuf.at[pl.ds(0, 448), :], ag_ss)
    all_sent(wbuf.at[pl.ds(0, 512), :], agp_ss)
    all_sent(attx.at[:, pl.ds(0, 896)], att_ss)
    all_sent(ga_s.at[:, pl.ds(0, 896)], ga_ss)
    all_sent(pbuf, rsp_ss)
    all_sent(wbuf.at[pl.ds(0, 224), :], rs_ss)
    all_sent(pw_s.at[:, pl.ds(0, NP - 1)], pw_ss)
    all_sent(pz_s.at[:, pl.ds(0, NZ - 1)], pz_ss)
    all_sent(dh.at[:, pl.ds(0, 896), :], d_ss)
    all_sent(wgp_s.at[1, pl.ds(0, NP - 1)], wgp_ss)
    all_sent(ta.at[pl.ds(0, NP - 1)], ta_ss)
    all_sent(tb.at[pl.ds(0, NZ - 1)], tb_ss)
    all_sent(tc.at[pl.ds(0, NP - 1)], tc_ss)
    tp_copy().wait_send()

    @pl.when(f > 0)
    def _():
        go_down().wait_send()

    @pl.when(f < FS - 1)
    def _():
        go_up().wait_send()


def put_out(*refs):
    sources, targets, sems = refs[:6], refs[6:12], refs[12]
    copies = [pltpu.make_async_copy(sources[i], targets[i], sems.at[i]) for i in range(6)]
    for copy in copies:
        copy.start()
    for copy in copies:
        copy.wait()


def shards(queries, key_rows, value_rows, out_weight, conv_weight, grad_out):
    vmem = pl.BlockSpec(memory_space=pltpu.VMEM)
    hbm = pl.BlockSpec(memory_space=pltpu.HBM)
    anywhere = pl.BlockSpec(memory_space=pl.ANY)
    dma = pltpu.SemaphoreType.DMA
    results = (
        ((ROWS, D), BF16),
        ((ROWS, INNER), BF16),
        ((ROWS, INNER), BF16),
        ((ROWS, INNER), BF16),
        ((4, D), F32),
        ((KERNEL, D), F32),
    )
    shapes = tuple(jax.ShapeDtypeStruct(*result) for result in results)
    found = pl.pallas_call(
        kernel,
        out_shape=shapes,
        in_specs=[hbm] * 6,
        out_specs=(vmem,) * 6,
        scratch_shapes=[
            pltpu.VMEM((3, SPAN, HDIM), BF16),
            pltpu.VMEM((SPAN, SPAN), BF16),
            pltpu.VMEM((SPAN + 2 * HALO, HDIM), BF16),
            pltpu.VMEM((ROWS + 2 * HALO, INNER), BF16),
            pltpu.VMEM((NP, 4, D), BF16),
            pltpu.VMEM((64, D), F32),
            pltpu.VMEM((INNER, D), BF16),
            pltpu.VMEM((INNER, INNER), BF16),
            pltpu.VMEM((ROWS + 2 * HALO, INNER), BF16),
            pltpu.VMEM((INNER, ROWS), BF16),
            pltpu.VMEM((160, D), BF16),
            pltpu.VMEM((KERNEL, D), BF16),
            pltpu.VMEM((KERNEL, 8, D), F32),
            pltpu.VMEM((ROWS + 2 * HALO, COLS), F32),
            pltpu.VMEM((ROWS + 2 * HALO, COLS), F32),
            pltpu.VMEM((ROWS + 2 * HALO, D), F32),
            pltpu.VMEM((160, COLS), F32),
            pltpu.VMEM((ROWS, D), F32),
            pltpu.VMEM((ROWS, COLS), BF16),
            pltpu.VMEM((ROWS, COLS), BF16),
            pltpu.VMEM((INNER, D), BF16),
            pltpu.VMEM((ROWS, INNER), F32),
            pltpu.VMEM((ROWS, INNER), BF16),
            pltpu.VMEM((SPAN, HDIM), BF16),
            pltpu.VMEM((3, SPAN, HDIM), BF16),
            pltpu.VMEM((SPAN, HDIM), F32),
            pltpu.VMEM((SPAN, HDIM), F32),
            pltpu.VMEM((512, D), BF16),
            pltpu.VMEM((2, 4, 64, D), BF16),
            pltpu.VMEM((2, 4, 64, D), BF16),
            pltpu.VMEM((2, NP, 4, 1024), BF16),
            pltpu.VMEM((2, NP, 4, 1024), BF16),
            pltpu.VMEM((2, NP, NZ, 4, PART), BF16),
            pltpu.VMEM((2, NP, NZ, 4, PART), BF16),
            pltpu.VMEM((2, NZ, 4, PART), BF16),
            pltpu.VMEM((2, NZ, 4, PART), BF16),
            pltpu.VMEM((32, D), F32),
            pltpu.VMEM((NP, 32, 128), F32),
            pltpu.VMEM((32, 128), F32),
            pltpu.VMEM((32, 128), F32),
            pltpu.VMEM((NZ, 32, 128), BF16),
            pltpu.VMEM((32, 128), BF16),
            pltpu.VMEM((NP, 32, 128), BF16),
            dma((6,)),
            dma, dma((FS,)), dma((2,)),
            dma, dma,
            dma((2,)), dma((2,)),
            dma, dma((2, 4, 4)),
            dma, dma((4,)),
            dma, dma,
            dma, dma,
            dma, dma((4,)),
            dma, dma((2, 4, 4)),
            dma, dma((3,)),
            dma, dma((2,)),
            dma, dma((2,)),
            dma, dma((2,)),
            dma, dma,
            dma, dma,
            dma, dma,
            dma, dma,
        ],
        compiler_params=pltpu.CompilerParams(
            collective_id=0, has_side_effects=True, vmem_limit_bytes=50 * 1024 * 1024
        ),
    )(
        *(
            pltpu.with_memory_space_constraint(given, pltpu.HBM)
            for given in (queries[0], key_rows[0], value_rows[0], out_weight, conv_weight, grad_out[0])
        )
    )
    block_out, grad_queries, grad_keys, grad_values, weight_grad, conv_grad = pl.pallas_call(
        put_out,
        out_shape=shapes,
        in_specs=[anywhere] * 6,
        out_specs=(hbm,) * 6,
        scratch_shapes=[dma((6,))],
        compiler_params=pltpu.CompilerParams(vmem_limit_bytes=8 * 1024 * 1024),
    )(*found)
    return (block_out[None], grad_queries[None], grad_keys[None], grad_values[None], weight_grad, conv_grad)


def solution(mesh):
    return jax.shard_map(
        shards,
        mesh=mesh,
        in_specs=(
            P("frame", "fsdp", None),
            P("frame", "fsdp", None),
            P("frame", "fsdp", None),
            P(("fsdp", "frame"), None),
            P(),
            P("frame", "fsdp", None),
        ),
        out_specs=(
            P("frame", "fsdp", None),
            P("frame", "fsdp", None),
            P("frame", "fsdp", None),
            P("frame", "fsdp", None),
            P(("fsdp", "frame"), None),
            P(),
        ),
        check_vma=False,
    )
```
